512 devices in a mesh: day: 32 (over z, x), tile: 16 (over y, core).
Axes of the slice: x: 4, y: 8, z: 8, core: 2. Of those that a mesh axis runs over, the one named last changes fastest.
Arguments:
- causal: bfloat16 [32, 1, 1024, 1024], P('day', None, 'tile'), may hold values from -24 to 24
- acausal_held: bfloat16 [32, 1, 1024, 1024], P('day', None, 'tile'), may hold values from -24 to 24
- fk_bins: int32 [512, 1024], P('day'), may hold values from 0 to 7
- band_gain: float32 [8], replicated, may hold values from 0.1 to 1
Outputs:
- filtered: float32 [1024, 1, 1024], P('day', None, 'tile')
The draws below stay inside these ranges and needn't reach their ends.
All inputs are finite; a program needn't handle non-finite values.
Results may differ from the reference program's by a relative error of at most 0.0023.
Values may be sent and summed in bfloat16 or wider, within the bound.
No kernel may reach another device: no remote copies, remote signals or barrier semaphores. Data moves between devices by JAX's collectives and lax.ppermute only.
A program may use at most 64 MiB of HBM per device.

```python
import math
import jax
import jax.numpy as jnp
from jax import lax

SHOTS = 1
RECV = 1024
LAGH = 1024
NF = 512
NBANDS = 8
DAYS = 32


def with_ends(drawn, key, low, high):
    longest = drawn.shape.index(max(drawn.shape))
    spots = []
    for shift in (0, 1):
        where = [jax.random.randint(jax.random.fold_in(key, axis), (), 0, length) for axis, length in enumerate(drawn.shape)]
        where[longest] = (where[longest] + shift) % drawn.shape[longest]
        spots.append(tuple(where))
    return drawn.at[spots[0]].set(low).at[spots[1]].set(high)


def block_scale(key, extent, pieces, low, largest):
    def one(dim, blocks):
        steps = jax.random.uniform(jax.random.fold_in(jax.random.fold_in(key, 6), dim), (blocks,), jnp.float32, low / len(pieces), largest / len(pieces))
        return jnp.repeat(jnp.exp(steps), extent[dim] // blocks).reshape((-1,) + (1,) * (len(extent) - dim - 1))

    level = one(*pieces[0])
    for cut in pieces[1:]:
        level = level * one(*cut)
    return level


def centred(rng, shape, spread, most, cuts=(), held_as=jnp.bfloat16):
    loudness = block_scale(rng, shape, cuts, -0.22, 0.18) if cuts else 1.0
    values = jax.random.normal(rng, shape, jnp.float32) * spread * loudness
    return jnp.minimum(jnp.maximum(values, -most), most).astype(held_as)


def setup_inputs(seed: int = 0) -> dict:
    splits = jax.random.split(jax.random.key(seed), 5)
    causal = centred(splits[0], (DAYS, SHOTS, RECV, LAGH), 4.0, 24.0, ((0, 32), (2, 16)))
    acausal_held = centred(splits[1], (DAYS, SHOTS, RECV, LAGH), 4.0, 24.0, ((0, 32), (2, 16)))
    fk_bins = with_ends(jax.random.randint(splits[2], (NF, RECV), 0, NBANDS), jax.random.fold_in(splits[2], 1), 0, NBANDS - 1).astype(jnp.int32)
    band_gain = jnp.clip(jnp.exp(jax.random.uniform(splits[3], (NBANDS,), jnp.float32, math.log(0.1), math.log(1.0))), 0.1, 1.0)
    return dict(causal=causal, acausal_held=acausal_held, fk_bins=fk_bins, band_gain=band_gain)


def lag_table(freq_count, lag_count):
    freq = lax.iota(jnp.int32, freq_count)
    lags = lax.iota(jnp.int32, lag_count)
    phase = (freq[:, None] * lags[None, :] % lag_count).astype(jnp.float32) * (2.0 * math.pi / lag_count)
    basis_table = jnp.stack([jnp.cos(phase), -jnp.sin(phase)], axis=1) / math.sqrt(lag_count)
    return basis_table.astype(jnp.bfloat16).astype(jnp.float32)

def reference(causal, acausal_held, fk_bins, band_gain):
    days = causal.shape[0]
    acausal = jnp.roll(acausal_held, RECV // 2, axis=2)
    total = lax.optimization_barrier(jnp.sum(causal, axis=0, dtype=jnp.float32)) + lax.optimization_barrier(jnp.sum(acausal, axis=0, dtype=jnp.float32))
    basis_table = lag_table(NF, LAGH)
    spectra = jnp.einsum('fcl,srl->fcsr', basis_table, total, precision=lax.Precision.HIGHEST) / days
    real_part = spectra[:, 0]
    imaginary_part = spectra[:, 1]
    recv = lax.iota(jnp.int32, RECV)
    phase = (recv[:, None] * recv[None, :] % RECV).astype(jnp.float32) * (2.0 * math.pi / RECV)
    cosine_basis = jnp.cos(phase) / math.sqrt(RECV)
    sine_basis = jnp.sin(phase) / math.sqrt(RECV)
    upper_half = lax.Precision.HIGHEST
    waveform_real = jnp.einsum('zhy,yu->zhu', real_part, cosine_basis, precision=upper_half) + jnp.einsum('zhy,yu->zhu', imaginary_part, sine_basis, precision=upper_half)
    waveform_imaginary = jnp.einsum('zhy,yu->zhu', imaginary_part, cosine_basis, precision=upper_half) - jnp.einsum('zhy,yu->zhu', real_part, sine_basis, precision=upper_half)
    gains = band_gain[fk_bins][:, None, :]
    waveform_real = waveform_real * gains
    waveform_imaginary = waveform_imaginary * gains
    lines_real = jnp.einsum('vct,mt->vcm', waveform_real, cosine_basis, precision=upper_half) - jnp.einsum('vct,mt->vcm', waveform_imaginary, sine_basis, precision=upper_half)
    lines_imaginary = jnp.einsum('vct,mt->vcm', waveform_imaginary, cosine_basis, precision=upper_half) + jnp.einsum('vct,mt->vcm', waveform_real, sine_basis, precision=upper_half)
    lags = lax.iota(jnp.int32, LAGH)
    freq = lax.iota(jnp.int32, NF)
    angle = (lags[:, None] * freq[None, :] % LAGH).astype(jnp.float32) * (2.0 * math.pi / LAGH)
    weight = jnp.where(freq == 0, 1.0, 2.0).astype(jnp.float32)[None, :] / math.sqrt(LAGH)
    inverse_cosine_basis = weight * jnp.cos(angle)
    inverse_sine_basis = -weight * jnp.sin(angle)
    return jnp.einsum('hy,yon->hon', inverse_cosine_basis, lines_real, precision=upper_half) + jnp.einsum('hy,yon->hon', inverse_sine_basis, lines_imaginary, precision=upper_half)
```

```python
import functools
import math

import jax
import jax.numpy as jnp
import numpy as np
from jax import lax
from jax.experimental import pallas as pl
from jax.experimental.pallas import tpu as pltpu
from jax.sharding import PartitionSpec as P

HIGHEST = lax.Precision.HIGHEST


def lag_basis(freq_count, lag_count, owners):
    freq = np.arange(freq_count)
    phase = (freq[:, None] * np.arange(lag_count)[None, :] % lag_count) * (2.0 * np.pi / lag_count)
    table = np.stack([np.cos(phase), -np.sin(phase)], axis=0) / math.sqrt(lag_count)
    table = table.reshape(2, owners, freq_count // owners, lag_count).transpose(1, 0, 2, 3)
    return table.reshape(2 * freq_count, lag_count).astype(np.float32).astype(jnp.bfloat16)


def halves(real_part, imag_part):
    return np.concatenate([real_part, imag_part], axis=-1).astype(np.float32)


def block_dft(width, sign, scale):
    angle = (np.arange(width)[:, None] * np.arange(width)[None, :] % width) * (2.0 * np.pi / width)
    cosine, sine = np.cos(angle) * scale, sign * np.sin(angle) * scale
    return np.concatenate([halves(cosine, sine), halves(-sine, cosine)], axis=0)


def other_half(value):
    return pltpu.roll(value, value.shape[-1] // 2, value.ndim - 1)


def lag_kernel(table_ref, causal_ref, held_ref, out_ref):
    rows = jnp.concatenate([causal_ref[...], held_ref[...]], axis=0)
    out_ref[...] = lax.dot_general(
        table_ref[...], rows, (((1,), (1,)), ((), ())), preferred_element_type=jnp.float32
    ).astype(out_ref.dtype)


def stack_kernel(scale, parts_ref, out_ref):
    count = parts_ref.shape[0]
    total = parts_ref[0].astype(jnp.float32)
    for day in range(1, count):
        total = total + parts_ref[day].astype(jnp.float32)
    total = total * scale
    half = total.shape[0] // 2
    real_part, imag_part = total[:half], total[half:]
    low = lax.broadcasted_iota(jnp.int32, real_part.shape, 1) < real_part.shape[1] // 2
    causal = jnp.where(low, real_part, other_half(imag_part))
    held = jnp.where(low, other_half(real_part), imag_part)
    for peer in range(out_ref.shape[0]):
        out_ref[peer, :half] = causal
        out_ref[peer, half:] = held


def filter_kernel(
    lines_ref, gains_ref, fore_ref, back_ref, turn_ref, unturn_ref, out_ref, work_ref
):
    blocks = lines_ref.shape[0]
    half = lines_ref.shape[1] // 2
    shape = (half, lines_ref.shape[2])
    low = lax.broadcasted_iota(jnp.int32, shape, 1) < shape[1] // 2
    sign = jnp.where(low, 1.0, -1.0)

    def minus_i(value):
        return other_half(value) * sign

    def rotated(value, power):
        power %= 16
        if power == 0:
            return value
        cosine, sine = math.cos(math.pi * power / 8), math.sin(math.pi * power / 8)
        return value * cosine + minus_i(value) * sine

    def four(a, b, c, d):
        p, m, q, n = a + c, a - c, b + d, minus_i(b - d)
        return p + q, m + n, p - q, m - n

    data = [lines_ref[j, :half] + lines_ref[(j + blocks // 2) % blocks, half:] for j in range(blocks)]
    inner = [four(*(data[4 * a + b] for a in range(4))) for b in range(4)]
    for c in range(4):
        outer = four(*(rotated(inner[b][c], b * c) for b in range(4)))
        for d in range(4):
            q = c + 4 * d
            value = outer[d]
            work_ref[q * half : (q + 1) * half] = (
                value * turn_ref[0, q : q + 1] + other_half(value) * turn_ref[1, q : q + 1]
            )
    wave = jnp.dot(
        work_ref[...], fore_ref[...], precision=HIGHEST, preferred_element_type=jnp.float32
    )
    masked = wave * gains_ref[...]
    work_ref[...] = jnp.dot(
        masked, back_ref[...], precision=HIGHEST, preferred_element_type=jnp.float32
    )
    total = None
    for q in range(blocks):
        value = work_ref[q * half : (q + 1) * half]
        term = value * unturn_ref[0, q : q + 1] + other_half(value) * unturn_ref[1, q : q + 1]
        total = term if total is None else total + term
    for peer in range(out_ref.shape[0]):
        out_ref[peer] = total


def gather_kernel(lines_ref, table_ref, out_ref):
    both = jnp.dot(
        table_ref[...], lines_ref[...], precision=HIGHEST, preferred_element_type=jnp.float32
    )
    half, width = both.shape[0] // 2, both.shape[1] // 2
    out_ref[...] = both[:half, :width] + other_half(both[half:])[:, :width]


def body(causal, acausal_held, fk_bins, band_gain):
    _, _, width, lag_count = causal.shape
    days, tiles = lax.axis_size("day"), lax.axis_size("tile")
    freq_count = lag_count // 2
    freq_local = freq_count // days
    recv_count = width * tiles
    lag_local = lag_count // days
    lanes = 2 * width
    day, tile = lax.axis_index("day"), lax.axis_index("tile")

    steps = 4
    table = jnp.asarray(lag_basis(freq_count, lag_count, days))
    block = 2 * freq_count // steps
    spectra = pl.pallas_call(
        lag_kernel,
        grid=(steps,),
        in_specs=[
            pl.BlockSpec((block, lag_count), lambda s: (s, 0)),
            pl.BlockSpec((width, lag_count), lambda s: (0, 0)),
            pl.BlockSpec((width, lag_count), lambda s: (0, 0)),
        ],
        out_specs=pl.BlockSpec((block, lanes), lambda s: (s, 0)),
        out_shape=jax.ShapeDtypeStruct((2 * freq_count, lanes), jnp.bfloat16),
    )(table, causal.reshape(width, lag_count), acausal_held.reshape(width, lag_count))
    parts = lax.all_to_all(
        spectra.reshape(days, 2 * freq_local, lanes), "day", 0, 0, tiled=True
    )
    stacked = pl.pallas_call(
        functools.partial(stack_kernel, 1.0 / days),
        out_shape=jax.ShapeDtypeStruct((tiles, 2 * freq_local, lanes), jnp.float32),
    )(parts)

    levels = lax.iota(jnp.int32, band_gain.shape[0])
    ordered = fk_bins.reshape(freq_local, width, tiles).transpose(2, 0, 1)
    gains = jnp.sum(jnp.where(ordered[..., None] == levels, band_gain, 0.0), axis=-1)
    gains = jnp.concatenate([gains, gains], axis=-1).reshape(tiles * freq_local, lanes)
    residue = lax.iota(jnp.int32, tiles)
    recv = tile * width + lax.iota(jnp.int32, width)
    angle = (residue[:, None] * recv[None, :] % recv_count).astype(jnp.float32) * (
        2.0 * math.pi / recv_count
    )
    cosine, sine = jnp.cos(angle), jnp.sin(angle)
    unturn = jnp.stack(
        [jnp.concatenate([cosine, cosine], axis=1), jnp.concatenate([-sine, sine], axis=1)]
    )
    lag = day * lag_local + lax.iota(jnp.int32, lag_local)
    freq = lax.iota(jnp.int32, freq_count)
    angle = (lag[:, None] * freq[None, :] % lag_count).astype(jnp.float32) * (
        2.0 * math.pi / lag_count
    )
    weight = jnp.where(freq == 0, 1.0, 2.0).astype(jnp.float32)[None, :] / math.sqrt(lag_count)
    inverse_table = jnp.concatenate([weight * jnp.cos(angle), -weight * jnp.sin(angle)], axis=0)

    scale = 1.0 / math.sqrt(recv_count)
    turn_angle = np.arange(tiles)[:, None] * np.arange(width)[None, :] * (2.0 * np.pi / recv_count)
    turn = np.stack(
        [
            halves(np.cos(turn_angle), np.cos(turn_angle)),
            halves(np.sin(turn_angle), -np.sin(turn_angle)),
        ]
    )
    gathered = lax.all_to_all(stacked, "tile", 0, 0, tiled=True)
    lines = pl.pallas_call(
        filter_kernel,
        out_shape=jax.ShapeDtypeStruct((days, freq_local, lanes), jnp.float32),
        scratch_shapes=[pltpu.VMEM((tiles * freq_local, lanes), jnp.float32)],
    )(
        gathered,
        gains,
        jnp.asarray(block_dft(width, -1.0, scale)),
        jnp.asarray(block_dft(width, 1.0, scale)),
        jnp.asarray(turn),
        unturn,
    )
    returned = lax.all_to_all(lines, "day", 0, 0, tiled=True)
    filtered = pl.pallas_call(
        gather_kernel,
        out_shape=jax.ShapeDtypeStruct((lag_local, width), jnp.float32),
    )(returned.reshape(freq_count, lanes), inverse_table)
    return filtered.reshape(lag_local, 1, width)


def solution(mesh):
    return jax.shard_map(
        body,
        mesh=mesh,
        in_specs=(P("day", None, "tile", None), P("day", None, "tile", None), P("day", None), P()),
        out_specs=P("day", None, "tile"),
        check_vma=False,
    )
```

```python
import functools
import math

import jax
import jax.numpy as jnp
import numpy as np
from jax import lax
from jax.experimental import pallas as pl
from jax.experimental.pallas import tpu as pltpu
from jax.sharding import Mesh
from jax.sharding import PartitionSpec as P

AXES = ("day", "high", "low", "core")
SCALE = 2.0**46
TINY = 2.0**-125
VMEM = pl.BlockSpec(memory_space=pltpu.VMEM)
HBM = pl.BlockSpec(memory_space=pltpu.HBM)
PARAMS = pltpu.CompilerParams(vmem_limit_bytes=8 * 2**20)


def lag_basis(freq_count, lag_count, owners):
    freq = np.arange(freq_count)
    phase = (freq[:, None] * np.arange(lag_count)[None, :] % lag_count) * (2.0 * np.pi / lag_count)
    table = np.stack([np.cos(phase), -np.sin(phase)], axis=0) / math.sqrt(lag_count)
    table = table[:, :, : lag_count // 2].reshape(2, owners, freq_count // owners, lag_count // 2)
    table = table.transpose(1, 0, 2, 3).reshape(2 * freq_count, lag_count // 2)
    return table.astype(np.float32).astype(jnp.bfloat16)


def halves(real_part, imag_part):
    return np.concatenate([real_part, imag_part], axis=-1).astype(np.float32)


def block_dft(width, sign, scale):
    angle = (np.arange(width)[:, None] * np.arange(width)[None, :] % width) * (2.0 * np.pi / width)
    cosine, sine = np.cos(angle) * scale, sign * np.sin(angle) * scale
    return np.concatenate([halves(cosine, sine), halves(-sine, cosine)], axis=0)


def other_half(value):
    return pltpu.roll(value, value.shape[-1] // 2, value.ndim - 1)


def lag_kernel(
    table_hbm, causal_hbm, held_hbm, out_hbm, table_ref, rows_ref, out_ref, sems, out_sems
):
    pieces = out_sems.shape[0]
    width = causal_hbm.shape[0]
    size = table_ref.shape[0] // pieces
    half = table_ref.shape[1]
    inputs = [
        pltpu.make_async_copy(causal_hbm, rows_ref.at[pl.ds(0, width)], sems.at[pieces]),
        pltpu.make_async_copy(held_hbm, rows_ref.at[pl.ds(width, width)], sems.at[pieces + 1]),
    ]
    tables = [
        pltpu.make_async_copy(
            table_hbm.at[pl.ds(p * size, size)], table_ref.at[pl.ds(p * size, size)], sems.at[p]
        )
        for p in range(pieces)
    ]
    for copy in inputs + tables:
        copy.start()
    for copy in inputs:
        copy.wait()
    rows = rows_ref[...]
    sides = jnp.concatenate([rows[:, :half], rows[:, half:]], axis=0)
    lanes = 2 * width
    odd = lax.broadcasted_iota(jnp.int32, (size, lanes), 0) % 2
    sign = (1 - 2 * odd).astype(jnp.float32)
    outputs = []
    for p in range(pieces):
        tables[p].wait()
        both = lax.dot_general(
            table_ref[p * size : (p + 1) * size],
            sides,
            (((1,), (1,)), ((), ())),
            preferred_element_type=jnp.float32,
        )
        out_ref[p * size : (p + 1) * size] = (both[:, :lanes] + sign * both[:, lanes:]).astype(
            out_ref.dtype
        )
        outputs.append(
            pltpu.make_async_copy(
                out_ref.at[pl.ds(p * size, size)], out_hbm.at[pl.ds(p * size, size)], out_sems.at[p]
            )
        )
        outputs[p].start()
    for copy in outputs:
        copy.wait()


def coded(value):
    value = value * SCALE
    return (value * jnp.abs(value)).astype(jnp.bfloat16)


def decoded(code):
    code = code.astype(jnp.float32)
    return code * lax.rsqrt(jnp.maximum(jnp.abs(code), TINY)) * (1.0 / SCALE)


def split(value):
    high = value.astype(jnp.bfloat16)
    return high, (value - high.astype(jnp.float32)).astype(jnp.bfloat16)


def split_rows(matrix):
    high = matrix.astype(jnp.bfloat16)
    low = (matrix - high.astype(np.float32)).astype(jnp.bfloat16)
    return np.concatenate([high, high, low], axis=0)


def product(value, matrix):
    high, low = split(value)
    return jnp.dot(
        jnp.concatenate([high, low, high], axis=1), matrix, preferred_element_type=jnp.float32
    )


def stack_kernel(scale, parts_ref, out_ref):
    count, pairs = parts_ref.shape[0], parts_ref.shape[1]
    half = parts_ref.shape[2] // 2
    totals = [parts_ref[0, pair].astype(jnp.float32) for pair in range(pairs)]
    for day in range(1, count):
        totals = [totals[pair] + parts_ref[day, pair].astype(jnp.float32) for pair in range(pairs)]
    for pair in range(pairs):
        total = totals[pair] * scale
        real_part, imag_part = total[:half], total[half:]
        low = lax.broadcasted_iota(jnp.int32, real_part.shape, 1) < real_part.shape[1] // 2
        causal = jnp.where(low, real_part, other_half(imag_part))
        held = jnp.where(low, other_half(real_part), imag_part)
        code = coded(jnp.concatenate([causal, held], axis=0))
        for peer in range(out_ref.shape[0]):
            out_ref[peer, pair] = code


def filter_kernel(
    lines_ref, gains_ref, fore_ref, back_ref, turn_ref, unturn_ref, out_ref, work_ref
):
    peers, pairs, half, lanes = lines_ref.shape
    half //= 2
    blocks = peers * pairs
    low = lax.broadcasted_iota(jnp.int32, (half, lanes), 1) < lanes // 2
    sign = jnp.where(low, 1.0, -1.0)

    def minus_i(value):
        return other_half(value) * sign

    def rotated(value, power):
        power %= 16
        if power == 0:
            return value
        cosine, sine = math.cos(math.pi * power / 8), math.sin(math.pi * power / 8)
        return value * cosine + minus_i(value) * sine

    def four(a, b, c, d):
        p, m, q, n = a + c, a - c, b + d, minus_i(b - d)
        return p + q, m + n, p - q, m - n

    data = []
    value = decoded(lines_ref[...])
    for block in range(blocks):
        high, pair, core = block // (2 * pairs), block // 2 % pairs, block % 2
        peer = 2 * high + core
        data.append(value[peer, pair, :half] + value[(peer + peers // 2) % peers, pair, half:])
    inner = [four(*(data[4 * a + b] for a in range(4))) for b in range(4)]
    for c in range(4):
        outer = four(*(rotated(inner[b][c], b * c) for b in range(4)))
        for d in range(4):
            q = c + 4 * d
            value = outer[d]
            work_ref[q * half : (q + 1) * half] = (
                value * turn_ref[0, q : q + 1] + other_half(value) * turn_ref[1, q : q + 1]
            )
    wave = product(work_ref[...], fore_ref[...])
    work_ref[...] = product(wave * gains_ref[...], back_ref[...])
    for pair in range(pairs):
        total = None
        for q in range(blocks):
            value = work_ref[q * half : (q + 1) * half]
            term = value * unturn_ref[pair, 0, q : q + 1] + other_half(value) * unturn_ref[
                pair, 1, q : q + 1
            ]
            total = term if total is None else total + term
        code = coded(total)
        for day in range(out_ref.shape[0] // pairs):
            out_ref[day * pairs + pair] = code


def gather_kernel(codes_ref, table_ref, out_ref):
    owners, freqs, lanes = codes_ref.shape
    lines = decoded(codes_ref[...]).reshape(owners * freqs, lanes)
    line_high, line_low = split(lines)
    table_high, table_low = split(table_ref[...])
    rows, width = table_high.shape[0] // 2, lanes // 2
    both = jnp.dot(
        jnp.concatenate([table_high, table_low], axis=0),
        line_high,
        preferred_element_type=jnp.float32,
    )
    both = both[: 2 * rows] + both[2 * rows :]
    both = both + jnp.dot(table_high, line_low, preferred_element_type=jnp.float32)
    out_ref[...] = both[:rows, :width] + other_half(both[rows:])[:, :width]


def body(causal, acausal_held, fk_bins, band_gain):
    _, _, width, lag_count = causal.shape
    days, highs, pairs, cores = (lax.axis_size(name) for name in AXES)
    tiles = highs * pairs * cores
    owners = days * pairs
    freq_count = lag_count // 2
    freq_local = freq_count // owners
    recv_count = width * tiles
    lag_local = lag_count // days
    lanes = 2 * width
    day, high, pair, core = (lax.axis_index(name) for name in AXES)

    table = jnp.asarray(lag_basis(freq_count, lag_count, owners))
    pieces = 2
    spectra = pl.pallas_call(
        lag_kernel,
        in_specs=[HBM] * 3,
        out_specs=HBM,
        out_shape=jax.ShapeDtypeStruct((2 * freq_count, lanes), jnp.bfloat16),
        scratch_shapes=[
            pltpu.VMEM((2 * freq_count, lag_count // 2), jnp.bfloat16),
            pltpu.VMEM((lanes, lag_count), jnp.bfloat16),
            pltpu.VMEM((2 * freq_count, lanes), jnp.bfloat16),
            pltpu.SemaphoreType.DMA((pieces + 2,)),
            pltpu.SemaphoreType.DMA((pieces,)),
        ],
    )(table, causal.reshape(width, lag_count), acausal_held.reshape(width, lag_count))
    parts = lax.all_to_all(
        spectra.reshape(owners, 2 * freq_local, lanes), ("day", "low"), 0, 0, tiled=True
    )

    levels = lax.iota(jnp.int32, band_gain.shape[0])
    own_bins = lax.dynamic_slice_in_dim(fk_bins, pair * freq_local, freq_local, 0)
    ordered = own_bins.reshape(freq_local, width, tiles).transpose(2, 0, 1)
    gains = jnp.sum(jnp.where(ordered[..., None] == levels, band_gain, 0.0), axis=-1)
    gains = jnp.concatenate([gains, gains], axis=-1).reshape(tiles * freq_local, lanes)
    residue = lax.iota(jnp.int32, tiles)
    own_blocks = (high * pairs + lax.iota(jnp.int32, pairs)) * cores + core
    recv = own_blocks[:, None] * width + lax.iota(jnp.int32, width)[None, :]
    angle = (residue[None, :, None] * recv[:, None, :] % recv_count).astype(jnp.float32) * (
        2.0 * math.pi / recv_count
    )
    cosine, sine = jnp.cos(angle), jnp.sin(angle)
    unturn = jnp.stack(
        [jnp.concatenate([cosine, cosine], axis=2), jnp.concatenate([-sine, sine], axis=2)],
        axis=1,
    )
    lag = day * lag_local + lax.iota(jnp.int32, lag_local)
    freq = lax.iota(jnp.int32, freq_count)
    angle = (lag[:, None] * freq[None, :] % lag_count).astype(jnp.float32) * (
        2.0 * math.pi / lag_count
    )
    weight = jnp.where(freq == 0, 1.0, 2.0).astype(jnp.float32)[None, :] / math.sqrt(lag_count)
    inverse_table = jnp.concatenate([weight * jnp.cos(angle), -weight * jnp.sin(angle)], axis=0)
    parts, gains, unturn, inverse_table = lax.optimization_barrier(
        (parts, gains, unturn, inverse_table)
    )

    stacked = pl.pallas_call(
        functools.partial(stack_kernel, 1.0 / days),
        in_specs=[VMEM],
        out_specs=VMEM,
        compiler_params=PARAMS,
        out_shape=jax.ShapeDtypeStruct(
            (highs * cores, pairs, 2 * freq_local, lanes), jnp.bfloat16
        ),
    )(parts.reshape(days, pairs, 2 * freq_local, lanes))
    scale = 1.0 / math.sqrt(recv_count)
    turn_angle = np.arange(tiles)[:, None] * np.arange(width)[None, :] * (2.0 * np.pi / recv_count)
    turn = np.stack(
        [
            halves(np.cos(turn_angle), np.cos(turn_angle)),
            halves(np.sin(turn_angle), -np.sin(turn_angle)),
        ]
    )
    gathered = lax.all_to_all(stacked, ("high", "core"), 0, 0, tiled=True)
    lines = pl.pallas_call(
        filter_kernel,
        in_specs=[VMEM] * 6,
        out_specs=VMEM,
        compiler_params=PARAMS,
        out_shape=jax.ShapeDtypeStruct((owners, freq_local, lanes), jnp.bfloat16),
        scratch_shapes=[pltpu.VMEM((tiles * freq_local, lanes), jnp.float32)],
    )(
        gathered,
        gains,
        jnp.asarray(split_rows(block_dft(width, -1.0, scale))),
        jnp.asarray(split_rows(block_dft(width, 1.0, scale))),
        jnp.asarray(turn),
        unturn,
    )
    returned = lax.all_to_all(
        lines, ("day", "low"), 0, 0, tiled=True
    )
    filtered = pl.pallas_call(
        gather_kernel,
        in_specs=[VMEM] * 2,
        out_specs=VMEM,
        compiler_params=PARAMS,
        out_shape=jax.ShapeDtypeStruct((lag_local, width), jnp.float32),
    )(returned, inverse_table)
    return filtered.reshape(lag_local, 1, width)


def solution(mesh):
    days, tiles = mesh.devices.shape
    split = Mesh(mesh.devices.reshape(days, tiles // 4, 2, 2), AXES)
    tile = ("high", "low", "core")
    return jax.shard_map(
        body,
        mesh=split,
        in_specs=(P("day", None, tile, None), P("day", None, tile, None), P("day", None), P()),
        out_specs=P("day", None, tile),
        check_vma=False,
    )
```

```python
import functools
import math

import jax
import jax.numpy as jnp
import numpy as np
from jax import lax
from jax.experimental import pallas as pl
from jax.experimental.pallas import tpu as pltpu
from jax.sharding import Mesh
from jax.sharding import PartitionSpec as P

AXES = ("z", "x", "high", "low", "core")
SCALE = 2.0**46
TINY = 2.0**-125
VMEM = pl.BlockSpec(memory_space=pltpu.VMEM)
HBM = pl.BlockSpec(memory_space=pltpu.HBM)
PARAMS = pltpu.CompilerParams(vmem_limit_bytes=8 * 2**20)


def lag_basis(freq_count, lag_count, owners):
    freq = np.arange(freq_count)
    phase = (freq[:, None] * np.arange(lag_count)[None, :] % lag_count) * (2.0 * np.pi / lag_count)
    table = np.stack([np.cos(phase), -np.sin(phase)], axis=0) / math.sqrt(lag_count)
    table = table[:, :, : lag_count // 2].reshape(2, owners, freq_count // owners, lag_count // 2)
    table = table.transpose(1, 0, 2, 3).reshape(2 * freq_count, lag_count // 2)
    return table.astype(np.float32).astype(jnp.bfloat16)


def halves(real_part, imag_part):
    return np.concatenate([real_part, imag_part], axis=-1).astype(np.float32)


def block_dft(width, sign, scale):
    angle = (np.arange(width)[:, None] * np.arange(width)[None, :] % width) * (2.0 * np.pi / width)
    cosine, sine = np.cos(angle) * scale, sign * np.sin(angle) * scale
    return np.concatenate([halves(cosine, sine), halves(-sine, cosine)], axis=0)


def other_half(value):
    return pltpu.roll(value, value.shape[-1] // 2, value.ndim - 1)


def lag_kernel(
    table_hbm, causal_hbm, held_hbm, out_hbm, table_ref, rows_ref, out_ref, sems, out_sems
):
    pieces = out_sems.shape[0]
    width = causal_hbm.shape[0]
    size = table_ref.shape[0] // pieces
    half = table_ref.shape[1]
    inputs = [
        pltpu.make_async_copy(causal_hbm, rows_ref.at[pl.ds(0, width)], sems.at[pieces]),
        pltpu.make_async_copy(held_hbm, rows_ref.at[pl.ds(width, width)], sems.at[pieces + 1]),
    ]
    tables = [
        pltpu.make_async_copy(
            table_hbm.at[pl.ds(p * size, size)], table_ref.at[pl.ds(p * size, size)], sems.at[p]
        )
        for p in range(pieces)
    ]
    for copy in inputs + tables:
        copy.start()
    for copy in inputs:
        copy.wait()
    rows = rows_ref[...]
    sides = jnp.concatenate([rows[:, :half], rows[:, half:]], axis=0)
    lanes = 2 * width
    odd = lax.broadcasted_iota(jnp.int32, (size, lanes), 0) % 2
    sign = (1 - 2 * odd).astype(jnp.float32)
    outputs = []
    for p in range(pieces):
        tables[p].wait()
        both = lax.dot_general(
            table_ref[p * size : (p + 1) * size],
            sides,
            (((1,), (1,)), ((), ())),
            preferred_element_type=jnp.float32,
        )
        out_ref[p * size : (p + 1) * size] = (both[:, :lanes] + sign * both[:, lanes:]).astype(
            out_ref.dtype
        )
        outputs.append(
            pltpu.make_async_copy(
                out_ref.at[pl.ds(p * size, size)], out_hbm.at[pl.ds(p * size, size)], out_sems.at[p]
            )
        )
        outputs[p].start()
    for copy in outputs:
        copy.wait()


def coded(value):
    value = value * SCALE
    return (value * jnp.abs(value)).astype(jnp.bfloat16)


def decoded(code):
    code = code.astype(jnp.float32)
    return code * lax.rsqrt(jnp.maximum(jnp.abs(code), TINY)) * (1.0 / SCALE)


def split(value):
    high = value.astype(jnp.bfloat16)
    return high, (value - high.astype(jnp.float32)).astype(jnp.bfloat16)


def split_rows(matrix):
    high = matrix.astype(jnp.bfloat16)
    low = (matrix - high.astype(np.float32)).astype(jnp.bfloat16)
    return np.concatenate([high, high, low], axis=0)


def product(value, matrix):
    high, low = split(value)
    return jnp.dot(
        jnp.concatenate([high, low, high], axis=1), matrix, preferred_element_type=jnp.float32
    )


def stack_kernel(scale, parts_ref, out_ref):
    count, pairs = parts_ref.shape[0], parts_ref.shape[1]
    half = parts_ref.shape[2] // 2
    totals = [parts_ref[0, pair].astype(jnp.float32) for pair in range(pairs)]
    for day in range(1, count):
        totals = [totals[pair] + parts_ref[day, pair].astype(jnp.float32) for pair in range(pairs)]
    for pair in range(pairs):
        total = totals[pair] * scale
        real_part, imag_part = total[:half], total[half:]
        low = lax.broadcasted_iota(jnp.int32, real_part.shape, 1) < real_part.shape[1] // 2
        causal = jnp.where(low, real_part, other_half(imag_part))
        held = jnp.where(low, other_half(real_part), imag_part)
        code = coded(jnp.concatenate([causal, held], axis=0))
        for peer in range(out_ref.shape[0]):
            out_ref[peer, pair] = code


def filter_kernel(
    lines_ref, gains_ref, fore_ref, back_ref, turn_ref, unturn_ref, out_ref, work_ref
):
    peers, pairs, half, lanes = lines_ref.shape
    half //= 2
    blocks = peers * pairs
    low = lax.broadcasted_iota(jnp.int32, (half, lanes), 1) < lanes // 2
    sign = jnp.where(low, 1.0, -1.0)

    def minus_i(value):
        return other_half(value) * sign

    def rotated(value, power):
        power %= 16
        if power == 0:
            return value
        cosine, sine = math.cos(math.pi * power / 8), math.sin(math.pi * power / 8)
        return value * cosine + minus_i(value) * sine

    def four(a, b, c, d):
        p, m, q, n = a + c, a - c, b + d, minus_i(b - d)
        return p + q, m + n, p - q, m - n

    data = []
    value = decoded(lines_ref[...])
    for block in range(blocks):
        high, pair, core = block // (2 * pairs), block // 2 % pairs, block % 2
        highs = peers // 2
        peer, other = core * highs + high, core * highs + (high + highs // 2) % highs
        data.append(value[peer, pair, :half] + value[other, pair, half:])
    inner = [four(*(data[4 * a + b] for a in range(4))) for b in range(4)]
    for c in range(4):
        outer = four(*(rotated(inner[b][c], b * c) for b in range(4)))
        for d in range(4):
            q = c + 4 * d
            value = outer[d]
            work_ref[q * half : (q + 1) * half] = (
                value * turn_ref[0, q : q + 1] + other_half(value) * turn_ref[1, q : q + 1]
            )
    wave = product(work_ref[...], fore_ref[...])
    work_ref[...] = product(wave * gains_ref[...], back_ref[...])
    for pair in range(pairs):
        total = None
        for q in range(blocks):
            value = work_ref[q * half : (q + 1) * half]
            term = value * unturn_ref[pair, 0, q : q + 1] + other_half(value) * unturn_ref[
                pair, 1, q : q + 1
            ]
            total = term if total is None else total + term
        code = coded(total)
        for day in range(out_ref.shape[0] // pairs):
            out_ref[day * pairs + pair] = code


def gather_kernel(codes_ref, table_ref, out_ref):
    owners, freqs, lanes = codes_ref.shape
    rows, width = table_ref.shape[0] // 4, lanes // 2
    chunks = 2
    size = owners // chunks
    total = None
    for c in range(chunks):
        lines = decoded(codes_ref[c * size : (c + 1) * size]).reshape(size * freqs, lanes)
        line_high, line_low = split(lines)
        table = table_ref[:, c * size * freqs : (c + 1) * size * freqs]
        both = jnp.dot(table, line_high, preferred_element_type=jnp.float32)
        both = both[: 2 * rows] + both[2 * rows :]
        both = both + jnp.dot(table[: 2 * rows], line_low, preferred_element_type=jnp.float32)
        total = both if total is None else total + both
    out_ref[...] = total[:rows, :width] + other_half(total[rows:])[:, :width]


def body(causal, acausal_held, fk_bins, band_gain):
    _, _, width, lag_count = causal.shape
    depth, breadth, highs, pairs, cores = (lax.axis_size(name) for name in AXES)
    days = depth * breadth
    tiles = highs * pairs * cores
    owners = days * pairs
    freq_count = lag_count // 2
    freq_local = freq_count // owners
    recv_count = width * tiles
    lag_local = lag_count // days
    lanes = 2 * width
    z, x, high, pair, core = (lax.axis_index(name) for name in AXES)
    day = z * breadth + x

    table = jnp.asarray(lag_basis(freq_count, lag_count, owners))
    pieces = 1
    spectra = pl.pallas_call(
        lag_kernel,
        in_specs=[HBM] * 3,
        out_specs=HBM,
        out_shape=jax.ShapeDtypeStruct((2 * freq_count, lanes), jnp.bfloat16),
        scratch_shapes=[
            pltpu.VMEM((2 * freq_count, lag_count // 2), jnp.bfloat16),
            pltpu.VMEM((lanes, lag_count), jnp.bfloat16),
            pltpu.VMEM((2 * freq_count, lanes), jnp.bfloat16),
            pltpu.SemaphoreType.DMA((pieces + 2,)),
            pltpu.SemaphoreType.DMA((pieces,)),
        ],
    )(table, causal.reshape(width, lag_count), acausal_held.reshape(width, lag_count))
    parts = lax.all_to_all(
        spectra.reshape(owners, 2 * freq_local, lanes), ("z", "x", "low"), 0, 0, tiled=True
    )

    levels = lax.iota(jnp.int32, band_gain.shape[0])
    own_bins = lax.dynamic_slice_in_dim(fk_bins, pair * freq_local, freq_local, 0)
    ordered = own_bins.reshape(freq_local, width, tiles).transpose(2, 0, 1)
    gains = jnp.sum(jnp.where(ordered[..., None] == levels, band_gain, 0.0), axis=-1)
    gains = jnp.concatenate([gains, gains], axis=-1).reshape(tiles * freq_local, lanes)
    residue = lax.iota(jnp.int32, tiles)
    own_blocks = (high * pairs + lax.iota(jnp.int32, pairs)) * cores + core
    recv = own_blocks[:, None] * width + lax.iota(jnp.int32, width)[None, :]
    angle = (residue[None, :, None] * recv[:, None, :] % recv_count).astype(jnp.float32) * (
        2.0 * math.pi / recv_count
    )
    cosine, sine = jnp.cos(angle), jnp.sin(angle)
    unturn = jnp.stack(
        [jnp.concatenate([cosine, cosine], axis=2), jnp.concatenate([-sine, sine], axis=2)],
        axis=1,
    )
    lag = day * lag_local + lax.iota(jnp.int32, lag_local)
    freq = np.arange(freq_count, dtype=np.int32).reshape(depth, breadth, -1)
    freq = jnp.asarray(freq.transpose(1, 0, 2).reshape(-1))
    angle = (lag[:, None] * freq[None, :] % lag_count).astype(jnp.float32) * (
        2.0 * math.pi / lag_count
    )
    weight = jnp.where(freq == 0, 1.0, 2.0).astype(jnp.float32)[None, :] / math.sqrt(lag_count)
    inverse_table = jnp.concatenate([weight * jnp.cos(angle), -weight * jnp.sin(angle)], axis=0)
    table_high = lax.reduce_precision(inverse_table, 8, 7)
    inverse_table = jnp.concatenate([table_high, inverse_table - table_high], axis=0)
    inverse_table = inverse_table.astype(jnp.bfloat16)
    parts, gains, unturn, inverse_table = lax.optimization_barrier(
        (parts, gains, unturn, inverse_table)
    )

    stacked = pl.pallas_call(
        functools.partial(stack_kernel, 1.0 / days),
        in_specs=[VMEM],
        out_specs=VMEM,
        compiler_params=PARAMS,
        out_shape=jax.ShapeDtypeStruct(
            (highs * cores, pairs, 2 * freq_local, lanes), jnp.bfloat16
        ),
    )(parts.reshape(days, pairs, 2 * freq_local, lanes))
    scale = 1.0 / math.sqrt(recv_count)
    turn_angle = np.arange(tiles)[:, None] * np.arange(width)[None, :] * (2.0 * np.pi / recv_count)
    turn = np.stack(
        [
            halves(np.cos(turn_angle), np.cos(turn_angle)),
            halves(np.sin(turn_angle), -np.sin(turn_angle)),
        ]
    )
    gathered = lax.all_to_all(stacked, ("core", "high"), 0, 0, tiled=True)
    lines = pl.pallas_call(
        filter_kernel,
        in_specs=[VMEM] * 6,
        out_specs=VMEM,
        compiler_params=PARAMS,
        out_shape=jax.ShapeDtypeStruct((owners, freq_local, lanes), jnp.bfloat16),
        scratch_shapes=[pltpu.VMEM((tiles * freq_local, lanes), jnp.float32)],
    )(
        gathered,
        gains,
        jnp.asarray(split_rows(block_dft(width, -1.0, scale))),
        jnp.asarray(split_rows(block_dft(width, 1.0, scale))),
        jnp.asarray(turn),
        unturn,
    )
    returned = lax.all_to_all(
        lines, ("x", "z", "low"), 0, 0, tiled=True
    )
    filtered = pl.pallas_call(
        gather_kernel,
        in_specs=[VMEM] * 2,
        out_specs=VMEM,
        compiler_params=PARAMS,
        out_shape=jax.ShapeDtypeStruct((lag_local, width), jnp.float32),
    )(returned, inverse_table)
    return filtered.reshape(lag_local, 1, width)


def solution(mesh):
    days, tiles = mesh.devices.shape
    split = Mesh(mesh.devices.reshape(days // 4, 4, tiles // 2, 1, 2), AXES)
    day, tile = ("z", "x"), ("high", "low", "core")
    return jax.shard_map(
        body,
        mesh=split,
        in_specs=(P(day, None, tile, None), P(day, None, tile, None), P(day, None), P()),
        out_specs=P(day, None, tile),
        check_vma=False,
    )
```

```python
import functools
import math

import jax
import jax.numpy as jnp
import numpy as np
from jax import lax
from jax.experimental import pallas as pl
from jax.experimental.pallas import tpu as pltpu
from jax.sharding import Mesh
from jax.sharding import PartitionSpec as P

AXES = ("z", "x", "high", "low", "core")
SCALE = 2.0**46
TINY = 2.0**-125
VMEM = pl.BlockSpec(memory_space=pltpu.VMEM)
HBM = pl.BlockSpec(memory_space=pltpu.HBM)
PARAMS = pltpu.CompilerParams(vmem_limit_bytes=8 * 2**20)


def lag_basis(freq_count, lag_count, owners):
    freq = np.arange(freq_count)
    phase = (freq[:, None] * np.arange(lag_count)[None, :] % lag_count) * (2.0 * np.pi / lag_count)
    table = np.stack([np.cos(phase), -np.sin(phase)], axis=0) / math.sqrt(lag_count)
    table = table[:, :, : lag_count // 2].reshape(2, owners, freq_count // owners, lag_count // 2)
    table = table.transpose(1, 0, 2, 3).reshape(2 * freq_count, lag_count // 2)
    return table.astype(np.float32).astype(jnp.bfloat16)


def halves(real_part, imag_part):
    return np.concatenate([real_part, imag_part], axis=-1).astype(np.float32)


def block_dft(width, sign, scale):
    angle = (np.arange(width)[:, None] * np.arange(width)[None, :] % width) * (2.0 * np.pi / width)
    cosine, sine = np.cos(angle) * scale, sign * np.sin(angle) * scale
    return np.concatenate([halves(cosine, sine), halves(-sine, cosine)], axis=0)


def other_half(value):
    return pltpu.roll(value, value.shape[-1] // 2, value.ndim - 1)


def lag_kernel(
    table_hbm, causal_hbm, held_hbm, out_ref, table_ref, rows_ref, sems
):
    pieces = sems.shape[0] - 2
    width = causal_hbm.shape[0]
    size = table_ref.shape[0] // pieces
    half = table_ref.shape[1]
    inputs = [
        pltpu.make_async_copy(causal_hbm, rows_ref.at[pl.ds(0, width)], sems.at[pieces]),
        pltpu.make_async_copy(held_hbm, rows_ref.at[pl.ds(width, width)], sems.at[pieces + 1]),
    ]
    tables = [
        pltpu.make_async_copy(
            table_hbm.at[pl.ds(p * size, size)], table_ref.at[pl.ds(p * size, size)], sems.at[p]
        )
        for p in range(pieces)
    ]
    for copy in inputs + tables:
        copy.start()
    for copy in inputs:
        copy.wait()
    rows = rows_ref[...]
    sides = jnp.concatenate([rows[:, :half], rows[:, half:]], axis=0)
    lanes = 2 * width
    odd = lax.broadcasted_iota(jnp.int32, (size, lanes), 0) % 2
    sign = (1 - 2 * odd).astype(jnp.float32)
    for p in range(pieces):
        tables[p].wait()
        both = lax.dot_general(
            table_ref[p * size : (p + 1) * size],
            sides,
            (((1,), (1,)), ((), ())),
            preferred_element_type=jnp.float32,
        )
        out_ref[p * size : (p + 1) * size] = (both[:, :lanes] + sign * both[:, lanes:]).astype(
            out_ref.dtype
        )


def coded(value):
    value = value * SCALE
    return (value * jnp.abs(value)).astype(jnp.bfloat16)


def decoded(code):
    code = code.astype(jnp.float32)
    return code * lax.rsqrt(jnp.maximum(jnp.abs(code), TINY)) * (1.0 / SCALE)


def split(value):
    high = value.astype(jnp.bfloat16)
    return high, (value - high.astype(jnp.float32)).astype(jnp.bfloat16)


def split_rows(matrix):
    high = matrix.astype(jnp.bfloat16)
    low = (matrix - high.astype(np.float32)).astype(jnp.bfloat16)
    return np.concatenate([high, high, low], axis=0)


def product(value, matrix):
    high, low = split(value)
    return jnp.dot(
        jnp.concatenate([high, low, high], axis=1), matrix, preferred_element_type=jnp.float32
    )


def stack_kernel(scale, parts_ref, out_ref):
    count, pairs = parts_ref.shape[0], parts_ref.shape[1]
    half = parts_ref.shape[2] // 2
    totals = [parts_ref[0, pair].astype(jnp.float32) for pair in range(pairs)]
    for day in range(1, count):
        totals = [totals[pair] + parts_ref[day, pair].astype(jnp.float32) for pair in range(pairs)]
    for pair in range(pairs):
        total = totals[pair] * scale
        real_part, imag_part = total[:half], total[half:]
        low = lax.broadcasted_iota(jnp.int32, real_part.shape, 1) < real_part.shape[1] // 2
        causal = jnp.where(low, real_part, other_half(imag_part))
        held = jnp.where(low, other_half(real_part), imag_part)
        code = coded(jnp.concatenate([causal, held], axis=0))
        for peer in range(out_ref.shape[0]):
            out_ref[peer, pair] = code


def filter_kernel(
    lines_ref, gains_ref, fore_ref, back_ref, turn_ref, unturn_ref, out_ref, work_ref
):
    peers, pairs, half, lanes = lines_ref.shape
    half //= 2
    blocks = peers * pairs
    low = lax.broadcasted_iota(jnp.int32, (half, lanes), 1) < lanes // 2
    sign = jnp.where(low, 1.0, -1.0)

    def minus_i(value):
        return other_half(value) * sign

    def rotated(value, power):
        power %= 16
        if power == 0:
            return value
        cosine, sine = math.cos(math.pi * power / 8), math.sin(math.pi * power / 8)
        return value * cosine + minus_i(value) * sine

    def four(a, b, c, d):
        p, m, q, n = a + c, a - c, b + d, minus_i(b - d)
        return p + q, m + n, p - q, m - n

    data = []
    value = decoded(lines_ref[...])
    for block in range(blocks):
        high, pair, core = block // (2 * pairs), block // 2 % pairs, block % 2
        highs = peers // 2
        peer, other = core * highs + high, core * highs + (high + highs // 2) % highs
        data.append(value[peer, pair, :half] + value[other, pair, half:])
    inner = [four(*(data[4 * a + b] for a in range(4))) for b in range(4)]
    for c in range(4):
        outer = four(*(rotated(inner[b][c], b * c) for b in range(4)))
        for d in range(4):
            q = c + 4 * d
            value = outer[d]
            work_ref[q * half : (q + 1) * half] = (
                value * turn_ref[0, q : q + 1] + other_half(value) * turn_ref[1, q : q + 1]
            )
    wave = product(work_ref[...], fore_ref[...])
    work_ref[...] = product(wave * gains_ref[...], back_ref[...])
    for pair in range(pairs):
        total = None
        for q in range(blocks):
            value = work_ref[q * half : (q + 1) * half]
            term = value * unturn_ref[pair, 0, q : q + 1] + other_half(value) * unturn_ref[
                pair, 1, q : q + 1
            ]
            total = term if total is None else total + term
        code = coded(total)
        for day in range(out_ref.shape[0] // pairs):
            out_ref[day * pairs + pair] = code


def gather_kernel(codes_ref, table_ref, out_ref):
    owners, freqs, lanes = codes_ref.shape
    rows, width = table_ref.shape[0] // 4, lanes // 2
    chunks = 2
    size = owners // chunks
    total = None
    for c in range(chunks):
        lines = decoded(codes_ref[c * size : (c + 1) * size]).reshape(size * freqs, lanes)
        line_high, line_low = split(lines)
        table = table_ref[:, c * size * freqs : (c + 1) * size * freqs]
        both = jnp.dot(table, line_high, preferred_element_type=jnp.float32)
        both = both[: 2 * rows] + both[2 * rows :]
        both = both + jnp.dot(table[: 2 * rows], line_low, preferred_element_type=jnp.float32)
        total = both if total is None else total + both
    out_ref[...] = total[:rows, :width] + other_half(total[rows:])[:, :width]


def body(causal, acausal_held, fk_bins, band_gain):
    _, _, width, lag_count = causal.shape
    depth, breadth, highs, pairs, cores = (lax.axis_size(name) for name in AXES)
    days = depth * breadth
    tiles = highs * pairs * cores
    owners = days * pairs
    freq_count = lag_count // 2
    freq_local = freq_count // owners
    recv_count = width * tiles
    lag_local = lag_count // days
    lanes = 2 * width
    z, x, high, pair, core = (lax.axis_index(name) for name in AXES)
    day = z * breadth + x

    table = jnp.asarray(lag_basis(freq_count, lag_count, owners))
    pieces = 1
    spectra = pl.pallas_call(
        lag_kernel,
        in_specs=[HBM] * 3,
        out_specs=VMEM,
        compiler_params=PARAMS,
        out_shape=pltpu.VMEM((2 * freq_count, lanes), jnp.bfloat16),
        scratch_shapes=[
            pltpu.VMEM((2 * freq_count, lag_count // 2), jnp.bfloat16),
            pltpu.VMEM((lanes, lag_count), jnp.bfloat16),
            pltpu.SemaphoreType.DMA((pieces + 2,)),
        ],
    )(
        *(
            pltpu.with_memory_space_constraint(operand, pltpu.HBM)
            for operand in (
                table,
                causal.reshape(width, lag_count),
                acausal_held.reshape(width, lag_count),
            )
        )
    )
    parts = lax.all_to_all(
        spectra.reshape(owners, 2 * freq_local, lanes), ("z", "x", "low"), 0, 0, tiled=True
    )

    levels = lax.iota(jnp.int32, band_gain.shape[0])
    own_bins = lax.dynamic_slice_in_dim(fk_bins, pair * freq_local, freq_local, 0)
    ordered = own_bins.reshape(freq_local, width, tiles).transpose(2, 0, 1)
    gains = jnp.sum(jnp.where(ordered[..., None] == levels, band_gain, 0.0), axis=-1)
    gains = jnp.concatenate([gains, gains], axis=-1).reshape(tiles * freq_local, lanes)
    residue = lax.iota(jnp.int32, tiles)
    own_blocks = (high * pairs + lax.iota(jnp.int32, pairs)) * cores + core
    recv = own_blocks[:, None] * width + lax.iota(jnp.int32, width)[None, :]
    angle = (residue[None, :, None] * recv[:, None, :] % recv_count).astype(jnp.float32) * (
        2.0 * math.pi / recv_count
    )
    cosine, sine = jnp.cos(angle), jnp.sin(angle)
    unturn = jnp.stack(
        [jnp.concatenate([cosine, cosine], axis=2), jnp.concatenate([-sine, sine], axis=2)],
        axis=1,
    )
    lag = day * lag_local + lax.iota(jnp.int32, lag_local)
    freq = np.arange(freq_count, dtype=np.int32).reshape(depth, breadth, -1)
    freq = jnp.asarray(freq.transpose(1, 0, 2).reshape(-1))
    angle = (lag[:, None] * freq[None, :] % lag_count).astype(jnp.float32) * (
        2.0 * math.pi / lag_count
    )
    weight = jnp.where(freq == 0, 1.0, 2.0).astype(jnp.float32)[None, :] / math.sqrt(lag_count)
    inverse_table = jnp.concatenate([weight * jnp.cos(angle), -weight * jnp.sin(angle)], axis=0)
    table_high = lax.reduce_precision(inverse_table, 8, 7)
    inverse_table = jnp.concatenate([table_high, inverse_table - table_high], axis=0)
    inverse_table = inverse_table.astype(jnp.bfloat16)
    parts, gains, unturn, inverse_table = lax.optimization_barrier(
        (parts, gains, unturn, inverse_table)
    )

    stacked = pl.pallas_call(
        functools.partial(stack_kernel, 1.0 / days),
        in_specs=[VMEM],
        out_specs=VMEM,
        compiler_params=PARAMS,
        out_shape=jax.ShapeDtypeStruct(
            (highs * cores, pairs, 2 * freq_local, lanes), jnp.bfloat16
        ),
    )(parts.reshape(days, pairs, 2 * freq_local, lanes))
    scale = 1.0 / math.sqrt(recv_count)
    turn_angle = np.arange(tiles)[:, None] * np.arange(width)[None, :] * (2.0 * np.pi / recv_count)
    turn = np.stack(
        [
            halves(np.cos(turn_angle), np.cos(turn_angle)),
            halves(np.sin(turn_angle), -np.sin(turn_angle)),
        ]
    )
    gathered = lax.all_to_all(stacked, ("core", "high"), 0, 0, tiled=True)
    lines = pl.pallas_call(
        filter_kernel,
        in_specs=[VMEM] * 6,
        out_specs=VMEM,
        compiler_params=PARAMS,
        out_shape=jax.ShapeDtypeStruct((owners, freq_local, lanes), jnp.bfloat16),
        scratch_shapes=[pltpu.VMEM((tiles * freq_local, lanes), jnp.float32)],
    )(
        gathered,
        gains,
        jnp.asarray(split_rows(block_dft(width, -1.0, scale))),
        jnp.asarray(split_rows(block_dft(width, 1.0, scale))),
        jnp.asarray(turn),
        unturn,
    )
    returned = lax.all_to_all(
        lines, ("x", "z", "low"), 0, 0, tiled=True
    )
    filtered = pl.pallas_call(
        gather_kernel,
        in_specs=[VMEM] * 2,
        out_specs=VMEM,
        compiler_params=PARAMS,
        out_shape=jax.ShapeDtypeStruct((lag_local, width), jnp.float32),
    )(returned, inverse_table)
    return filtered.reshape(lag_local, 1, width)


def solution(mesh):
    days, tiles = mesh.devices.shape
    split = Mesh(mesh.devices.reshape(days // 4, 4, tiles // 2, 1, 2), AXES)
    day, tile = ("z", "x"), ("high", "low", "core")
    return jax.shard_map(
        body,
        mesh=split,
        in_specs=(P(day, None, tile, None), P(day, None, tile, None), P(day, None), P()),
        out_specs=P(day, None, tile),
        check_vma=False,
    )
```

```python
import functools
import math

import jax
import jax.numpy as jnp
import numpy as np
from jax import lax
from jax.experimental import pallas as pl
from jax.experimental.pallas import tpu as pltpu
from jax.sharding import Mesh
from jax.sharding import PartitionSpec as P

AXES = ("z", "x", "high", "low", "core")
SCALE = 2.0**46
TINY = 2.0**-125
VMEM = pl.BlockSpec(memory_space=pltpu.VMEM)
HBM = pl.BlockSpec(memory_space=pltpu.HBM)
PARAMS = pltpu.CompilerParams(vmem_limit_bytes=8 * 2**20)


def lag_basis(freq_count, lag_count, owners):
    freq = np.arange(freq_count)
    phase = (freq[:, None] * np.arange(lag_count)[None, :] % lag_count) * (2.0 * np.pi / lag_count)
    table = np.stack([np.cos(phase), -np.sin(phase)], axis=0) / math.sqrt(lag_count)
    table = table[:, :, : lag_count // 2].reshape(2, owners, freq_count // owners, lag_count // 2)
    table = table.transpose(1, 0, 2, 3).reshape(2 * freq_count, lag_count // 2)
    return table.astype(np.float32).astype(jnp.bfloat16)


def halves(real_part, imag_part):
    return np.concatenate([real_part, imag_part], axis=-1).astype(np.float32)


def block_dft(width, sign, scale):
    angle = (np.arange(width)[:, None] * np.arange(width)[None, :] % width) * (2.0 * np.pi / width)
    cosine, sine = np.cos(angle) * scale, sign * np.sin(angle) * scale
    return np.concatenate([halves(cosine, sine), halves(-sine, cosine)], axis=0)


def other_half(value):
    return pltpu.roll(value, value.shape[-1] // 2, value.ndim - 1)


def lag_kernel(
    table_hbm, causal_hbm, held_hbm, out_ref, table_ref, rows_ref, sems
):
    pieces = sems.shape[0] - 2
    width = causal_hbm.shape[0]
    size = table_ref.shape[0] // pieces
    half = table_ref.shape[1]
    inputs = [
        pltpu.make_async_copy(causal_hbm, rows_ref.at[pl.ds(0, width)], sems.at[pieces]),
        pltpu.make_async_copy(held_hbm, rows_ref.at[pl.ds(width, width)], sems.at[pieces + 1]),
    ]
    tables = [
        pltpu.make_async_copy(
            table_hbm.at[pl.ds(p * size, size)], table_ref.at[pl.ds(p * size, size)], sems.at[p]
        )
        for p in range(pieces)
    ]
    for copy in inputs + tables:
        copy.start()
    for copy in inputs:
        copy.wait()
    rows = rows_ref[...]
    sides = jnp.concatenate([rows[:, :half], rows[:, half:]], axis=0)
    lanes = 2 * width
    odd = lax.broadcasted_iota(jnp.int32, (size, lanes), 0) % 2
    sign = (1 - 2 * odd).astype(jnp.float32)
    for p in range(pieces):
        tables[p].wait()
        both = lax.dot_general(
            table_ref[p * size : (p + 1) * size],
            sides,
            (((1,), (1,)), ((), ())),
            preferred_element_type=jnp.float32,
        )
        out_ref[p * size : (p + 1) * size] = coded(both[:, :lanes] + sign * both[:, lanes:])


def coded(value):
    value = value * SCALE
    return (value * jnp.abs(value)).astype(jnp.bfloat16)


def decoded(code):
    code = code.astype(jnp.float32)
    return code * lax.rsqrt(jnp.maximum(jnp.abs(code), TINY)) * (1.0 / SCALE)


def split(value):
    high = value.astype(jnp.bfloat16)
    return high, (value - high.astype(jnp.float32)).astype(jnp.bfloat16)


def split_rows(matrix):
    high = matrix.astype(jnp.bfloat16)
    low = (matrix - high.astype(np.float32)).astype(jnp.bfloat16)
    return np.concatenate([high, high, low], axis=0)


def product(value, matrix):
    high, low = split(value)
    return jnp.dot(
        jnp.concatenate([high, low, high], axis=1), matrix, preferred_element_type=jnp.float32
    )


def stack_kernel(scale, parts_ref, out_ref):
    count, pairs = parts_ref.shape[0], parts_ref.shape[1]
    half = parts_ref.shape[2] // 2
    totals = [decoded(parts_ref[0, pair]) for pair in range(pairs)]
    for day in range(1, count):
        totals = [totals[pair] + decoded(parts_ref[day, pair]) for pair in range(pairs)]
    for pair in range(pairs):
        total = totals[pair] * scale
        real_part, imag_part = total[:half], total[half:]
        low = lax.broadcasted_iota(jnp.int32, real_part.shape, 1) < real_part.shape[1] // 2
        causal = jnp.where(low, real_part, other_half(imag_part))
        held = jnp.where(low, other_half(real_part), imag_part)
        code = coded(jnp.concatenate([causal, held], axis=0))
        for peer in range(out_ref.shape[0]):
            out_ref[peer, pair] = code


def filter_kernel(
    lines_ref, gains_ref, fore_ref, back_ref, turn_ref, unturn_ref, out_ref, work_ref
):
    peers, pairs, half, lanes = lines_ref.shape
    half //= 2
    blocks = peers * pairs
    low = lax.broadcasted_iota(jnp.int32, (half, lanes), 1) < lanes // 2
    sign = jnp.where(low, 1.0, -1.0)

    def minus_i(value):
        return other_half(value) * sign

    def rotated(value, power):
        power %= 16
        if power == 0:
            return value
        cosine, sine = math.cos(math.pi * power / 8), math.sin(math.pi * power / 8)
        return value * cosine + minus_i(value) * sine

    def four(a, b, c, d):
        p, m, q, n = a + c, a - c, b + d, minus_i(b - d)
        return p + q, m + n, p - q, m - n

    data = []
    value = decoded(lines_ref[...])
    for block in range(blocks):
        high, pair, core = block // (2 * pairs), block // 2 % pairs, block % 2
        highs = peers // 2
        peer, other = core * highs + high, core * highs + (high + highs // 2) % highs
        data.append(value[peer, pair, :half] + value[other, pair, half:])
    inner = [four(*(data[4 * a + b] for a in range(4))) for b in range(4)]
    for c in range(4):
        outer = four(*(rotated(inner[b][c], b * c) for b in range(4)))
        for d in range(4):
            q = c + 4 * d
            value = outer[d]
            work_ref[q * half : (q + 1) * half] = (
                value * turn_ref[0, q : q + 1] + other_half(value) * turn_ref[1, q : q + 1]
            )
    wave = product(work_ref[...], fore_ref[...])
    work_ref[...] = product(wave * gains_ref[...], back_ref[...])
    for pair in range(pairs):
        total = None
        for q in range(blocks):
            value = work_ref[q * half : (q + 1) * half]
            term = value * unturn_ref[pair, 0, q : q + 1] + other_half(value) * unturn_ref[
                pair, 1, q : q + 1
            ]
            total = term if total is None else total + term
        code = coded(total)
        for day in range(out_ref.shape[0] // pairs):
            out_ref[day * pairs + pair] = code


def gather_kernel(codes_ref, table_ref, out_ref):
    owners, freqs, lanes = codes_ref.shape
    rows, width = table_ref.shape[0] // 4, lanes // 2
    chunks = 2
    size = owners // chunks
    total = None
    for c in range(chunks):
        lines = decoded(codes_ref[c * size : (c + 1) * size]).reshape(size * freqs, lanes)
        line_high, line_low = split(lines)
        table = table_ref[:, c * size * freqs : (c + 1) * size * freqs]
        both = jnp.dot(table, line_high, preferred_element_type=jnp.float32)
        both = both[: 2 * rows] + both[2 * rows :]
        both = both + jnp.dot(table[: 2 * rows], line_low, preferred_element_type=jnp.float32)
        total = both if total is None else total + both
    out_ref[...] = total[:rows, :width] + other_half(total[rows:])[:, :width]


def body(causal, acausal_held, fk_bins, band_gain):
    _, _, width, lag_count = causal.shape
    depth, breadth, highs, pairs, cores = (lax.axis_size(name) for name in AXES)
    days = depth * breadth
    tiles = highs * pairs * cores
    owners = days * pairs
    freq_count = lag_count // 2
    freq_local = freq_count // owners
    recv_count = width * tiles
    lag_local = lag_count // days
    lanes = 2 * width
    z, x, high, pair, core = (lax.axis_index(name) for name in AXES)
    day = z * breadth + x

    table = jnp.asarray(lag_basis(freq_count, lag_count, owners))
    pieces = 1
    spectra = pl.pallas_call(
        lag_kernel,
        in_specs=[HBM] * 3,
        out_specs=VMEM,
        compiler_params=PARAMS,
        out_shape=pltpu.VMEM((2 * freq_count, lanes), jnp.bfloat16),
        scratch_shapes=[
            pltpu.VMEM((2 * freq_count, lag_count // 2), jnp.bfloat16),
            pltpu.VMEM((lanes, lag_count), jnp.bfloat16),
            pltpu.SemaphoreType.DMA((pieces + 2,)),
        ],
    )(
        *(
            pltpu.with_memory_space_constraint(operand, pltpu.HBM)
            for operand in (
                table,
                causal.reshape(width, lag_count),
                acausal_held.reshape(width, lag_count),
            )
        )
    )
    parts = lax.all_to_all(
        spectra.reshape(owners, 2 * freq_local, lanes), ("z", "x", "low"), 0, 0, tiled=True
    )

    levels = lax.iota(jnp.int32, band_gain.shape[0])
    own_bins = lax.dynamic_slice_in_dim(fk_bins, pair * freq_local, freq_local, 0)
    ordered = own_bins.reshape(freq_local, width, tiles).transpose(2, 0, 1)
    gains = jnp.sum(jnp.where(ordered[..., None] == levels, band_gain, 0.0), axis=-1)
    gains = jnp.concatenate([gains, gains], axis=-1).reshape(tiles * freq_local, lanes)
    residue = lax.iota(jnp.int32, tiles)
    own_blocks = (high * pairs + lax.iota(jnp.int32, pairs)) * cores + core
    recv = own_blocks[:, None] * width + lax.iota(jnp.int32, width)[None, :]
    angle = (residue[None, :, None] * recv[:, None, :] % recv_count).astype(jnp.float32) * (
        2.0 * math.pi / recv_count
    )
    cosine, sine = jnp.cos(angle), jnp.sin(angle)
    unturn = jnp.stack(
        [jnp.concatenate([cosine, cosine], axis=2), jnp.concatenate([-sine, sine], axis=2)],
        axis=1,
    )
    lag = day * lag_local + lax.iota(jnp.int32, lag_local)
    freq = np.arange(freq_count, dtype=np.int32).reshape(depth, breadth, -1)
    freq = jnp.asarray(freq.transpose(1, 0, 2).reshape(-1))
    angle = (lag[:, None] * freq[None, :] % lag_count).astype(jnp.float32) * (
        2.0 * math.pi / lag_count
    )
    weight = jnp.where(freq == 0, 1.0, 2.0).astype(jnp.float32)[None, :] / math.sqrt(lag_count)
    inverse_table = jnp.concatenate([weight * jnp.cos(angle), -weight * jnp.sin(angle)], axis=0)
    table_high = lax.reduce_precision(inverse_table, 8, 7)
    inverse_table = jnp.concatenate([table_high, inverse_table - table_high], axis=0)
    inverse_table = inverse_table.astype(jnp.bfloat16)
    parts, gains, unturn, inverse_table = lax.optimization_barrier(
        (parts, gains, unturn, inverse_table)
    )

    stacked = pl.pallas_call(
        functools.partial(stack_kernel, 1.0 / days),
        in_specs=[VMEM],
        out_specs=VMEM,
        compiler_params=PARAMS,
        out_shape=jax.ShapeDtypeStruct(
            (highs * cores, pairs, 2 * freq_local, lanes), jnp.bfloat16
        ),
    )(parts.reshape(days, pairs, 2 * freq_local, lanes))
    scale = 1.0 / math.sqrt(recv_count)
    turn_angle = np.arange(tiles)[:, None] * np.arange(width)[None, :] * (2.0 * np.pi / recv_count)
    turn = np.stack(
        [
            halves(np.cos(turn_angle), np.cos(turn_angle)),
            halves(np.sin(turn_angle), -np.sin(turn_angle)),
        ]
    )
    gathered = lax.all_to_all(stacked, ("core", "high"), 0, 0, tiled=True)
    lines = pl.pallas_call(
        filter_kernel,
        in_specs=[VMEM] * 6,
        out_specs=VMEM,
        compiler_params=PARAMS,
        out_shape=jax.ShapeDtypeStruct((owners, freq_local, lanes), jnp.bfloat16),
        scratch_shapes=[pltpu.VMEM((tiles * freq_local, lanes), jnp.float32)],
    )(
        gathered,
        gains,
        jnp.asarray(split_rows(block_dft(width, -1.0, scale))),
        jnp.asarray(split_rows(block_dft(width, 1.0, scale))),
        jnp.asarray(turn),
        unturn,
    )
    returned = lax.all_to_all(
        lines, ("x", "z", "low"), 0, 0, tiled=True
    )
    filtered = pl.pallas_call(
        gather_kernel,
        in_specs=[VMEM] * 2,
        out_specs=VMEM,
        compiler_params=PARAMS,
        out_shape=jax.ShapeDtypeStruct((lag_local, width), jnp.float32),
    )(returned, inverse_table)
    return filtered.reshape(lag_local, 1, width)


def solution(mesh):
    days, tiles = mesh.devices.shape
    split = Mesh(mesh.devices.reshape(days // 4, 4, tiles // 2, 1, 2), AXES)
    day, tile = ("z", "x"), ("high", "low", "core")
    return jax.shard_map(
        body,
        mesh=split,
        in_specs=(P(day, None, tile, None), P(day, None, tile, None), P(day, None), P()),
        out_specs=P(day, None, tile),
        check_vma=False,
    )
```

```python
import functools
import math

import jax
import jax.numpy as jnp
import numpy as np
from jax import lax
from jax.experimental import pallas as pl
from jax.experimental.pallas import tpu as pltpu
from jax.sharding import Mesh
from jax.sharding import PartitionSpec as P

AXES = ("z", "x", "high", "low", "core")
SCALE = 2.0**46
TINY = 2.0**-125
VMEM = pl.BlockSpec(memory_space=pltpu.VMEM)
HBM = pl.BlockSpec(memory_space=pltpu.HBM)
PARAMS = pltpu.CompilerParams(vmem_limit_bytes=8 * 2**20)


def lag_basis(freq_count, lag_count, depth, breadth, pairs):
    freq = np.arange(freq_count)
    phase = (freq[:, None] * np.arange(lag_count)[None, :] % lag_count) * (2.0 * np.pi / lag_count)
    table = np.stack([np.cos(phase), -np.sin(phase)], axis=0) / math.sqrt(lag_count)
    table = table[:, :, : lag_count // 2].reshape(2, depth, breadth, pairs, -1, lag_count // 2)
    table = table.transpose(2, 1, 3, 0, 4, 5).reshape(2 * freq_count, lag_count // 2)
    return table.astype(np.float32).astype(jnp.bfloat16)


def halves(real_part, imag_part):
    return np.concatenate([real_part, imag_part], axis=-1).astype(np.float32)


def block_dft(width, sign, scale):
    angle = (np.arange(width)[:, None] * np.arange(width)[None, :] % width) * (2.0 * np.pi / width)
    cosine, sine = np.cos(angle) * scale, sign * np.sin(angle) * scale
    return np.concatenate([halves(cosine, sine), halves(-sine, cosine)], axis=0)


def other_half(value):
    return pltpu.roll(value, value.shape[-1] // 2, value.ndim - 1)


def lag_kernel(
    table_hbm, causal_hbm, held_hbm, out_ref, table_ref, rows_ref, sems
):
    pieces = sems.shape[0] - 2
    width = causal_hbm.shape[0]
    size = table_ref.shape[0] // pieces
    half = table_ref.shape[1]
    inputs = [
        pltpu.make_async_copy(causal_hbm, rows_ref.at[pl.ds(0, width)], sems.at[pieces]),
        pltpu.make_async_copy(held_hbm, rows_ref.at[pl.ds(width, width)], sems.at[pieces + 1]),
    ]
    tables = [
        pltpu.make_async_copy(
            table_hbm.at[pl.ds(p * size, size)], table_ref.at[pl.ds(p * size, size)], sems.at[p]
        )
        for p in range(pieces)
    ]
    for copy in inputs + tables:
        copy.start()
    for copy in inputs:
        copy.wait()
    rows = rows_ref[...]
    sides = jnp.concatenate([rows[:, :half], rows[:, half:]], axis=0)
    lanes = 2 * width
    odd = lax.broadcasted_iota(jnp.int32, (size, lanes), 0) % 2
    sign = (1 - 2 * odd).astype(jnp.float32)
    for p in range(pieces):
        tables[p].wait()
        both = lax.dot_general(
            table_ref[p * size : (p + 1) * size],
            sides,
            (((1,), (1,)), ((), ())),
            preferred_element_type=jnp.float32,
        )
        out_ref[p * size : (p + 1) * size] = coded(both[:, :lanes] + sign * both[:, lanes:])


def coded(value):
    value = value * SCALE
    return (value * jnp.abs(value)).astype(jnp.bfloat16)


def decoded(code):
    code = code.astype(jnp.float32)
    return code * lax.rsqrt(jnp.maximum(jnp.abs(code), TINY)) * (1.0 / SCALE)


def split(value):
    high = value.astype(jnp.bfloat16)
    return high, (value - high.astype(jnp.float32)).astype(jnp.bfloat16)


def split_rows(matrix):
    high = matrix.astype(jnp.bfloat16)
    low = (matrix - high.astype(np.float32)).astype(jnp.bfloat16)
    return np.concatenate([high, high, low], axis=0)


def product(value, matrix):
    high, low = split(value)
    return jnp.dot(
        jnp.concatenate([high, low, high], axis=1), matrix, preferred_element_type=jnp.float32
    )


def stack_kernel(scale, parts_ref, out_ref):
    count, pairs = parts_ref.shape[0], parts_ref.shape[1]
    half = parts_ref.shape[2] // 2
    totals = [decoded(parts_ref[0, pair]) for pair in range(pairs)]
    for day in range(1, count):
        totals = [totals[pair] + decoded(parts_ref[day, pair]) for pair in range(pairs)]
    for pair in range(pairs):
        total = totals[pair] * scale
        real_part, imag_part = total[:half], total[half:]
        low = lax.broadcasted_iota(jnp.int32, real_part.shape, 1) < real_part.shape[1] // 2
        causal = jnp.where(low, real_part, other_half(imag_part))
        held = jnp.where(low, other_half(real_part), imag_part)
        code = coded(jnp.concatenate([causal, held], axis=0))
        for peer in range(out_ref.shape[0]):
            out_ref[peer, pair] = code


def filter_kernel(
    lines_ref, gains_ref, fore_ref, back_ref, turn_ref, unturn_ref, out_ref, work_ref
):
    peers, pairs, half, lanes = lines_ref.shape
    half //= 2
    blocks = peers * pairs
    low = lax.broadcasted_iota(jnp.int32, (half, lanes), 1) < lanes // 2
    sign = jnp.where(low, 1.0, -1.0)

    def minus_i(value):
        return other_half(value) * sign

    def rotated(value, power):
        power %= 16
        if power == 0:
            return value
        cosine, sine = math.cos(math.pi * power / 8), math.sin(math.pi * power / 8)
        return value * cosine + minus_i(value) * sine

    def four(a, b, c, d):
        p, m, q, n = a + c, a - c, b + d, minus_i(b - d)
        return p + q, m + n, p - q, m - n

    data = []
    value = decoded(lines_ref[...])
    for block in range(blocks):
        high, pair, core = block // (2 * pairs), block // 2 % pairs, block % 2
        highs = peers // 2
        peer, other = core * highs + high, core * highs + (high + highs // 2) % highs
        data.append(value[peer, pair, :half] + value[other, pair, half:])
    inner = [four(*(data[4 * a + b] for a in range(4))) for b in range(4)]
    for c in range(4):
        outer = four(*(rotated(inner[b][c], b * c) for b in range(4)))
        for d in range(4):
            q = c + 4 * d
            value = outer[d]
            work_ref[q * half : (q + 1) * half] = (
                value * turn_ref[0, q : q + 1] + other_half(value) * turn_ref[1, q : q + 1]
            )
    wave = product(work_ref[...], fore_ref[...])
    work_ref[...] = product(wave * gains_ref[...], back_ref[...])
    for pair in range(pairs):
        total = None
        for q in range(blocks):
            value = work_ref[q * half : (q + 1) * half]
            term = value * unturn_ref[pair, 0, q : q + 1] + other_half(value) * unturn_ref[
                pair, 1, q : q + 1
            ]
            total = term if total is None else total + term
        code = coded(total)
        for day in range(out_ref.shape[0] // pairs):
            out_ref[day * pairs + pair] = code


def gather_kernel(codes_ref, table_ref, out_ref):
    owners, freqs, lanes = codes_ref.shape
    rows, width = table_ref.shape[0] // 4, lanes // 2
    chunks = 2
    size = owners // chunks
    total = None
    for c in range(chunks):
        lines = decoded(codes_ref[c * size : (c + 1) * size]).reshape(size * freqs, lanes)
        line_high, line_low = split(lines)
        table = table_ref[:, c * size * freqs : (c + 1) * size * freqs]
        both = jnp.dot(table, line_high, preferred_element_type=jnp.float32)
        both = both[: 2 * rows] + both[2 * rows :]
        both = both + jnp.dot(table[: 2 * rows], line_low, preferred_element_type=jnp.float32)
        total = both if total is None else total + both
    out_ref[...] = total[:rows, :width] + other_half(total[rows:])[:, :width]


def body(causal, acausal_held, fk_bins, band_gain):
    _, _, width, lag_count = causal.shape
    depth, breadth, highs, pairs, cores = (lax.axis_size(name) for name in AXES)
    days = depth * breadth
    tiles = highs * pairs * cores
    owners = days * pairs
    freq_count = lag_count // 2
    freq_local = freq_count // owners
    recv_count = width * tiles
    lag_local = lag_count // days
    lanes = 2 * width
    z, x, high, pair, core = (lax.axis_index(name) for name in AXES)
    day = z * breadth + x

    table = jnp.asarray(lag_basis(freq_count, lag_count, depth, breadth, pairs))
    pieces = 1
    spectra = pl.pallas_call(
        lag_kernel,
        in_specs=[HBM] * 3,
        out_specs=VMEM,
        compiler_params=PARAMS,
        out_shape=pltpu.VMEM((2 * freq_count, lanes), jnp.bfloat16),
        scratch_shapes=[
            pltpu.VMEM((2 * freq_count, lag_count // 2), jnp.bfloat16),
            pltpu.VMEM((lanes, lag_count), jnp.bfloat16),
            pltpu.SemaphoreType.DMA((pieces + 2,)),
        ],
    )(
        *(
            pltpu.with_memory_space_constraint(operand, pltpu.HBM)
            for operand in (
                table,
                causal.reshape(width, lag_count),
                acausal_held.reshape(width, lag_count),
            )
        )
    )
    parts = lax.all_to_all(
        spectra.reshape(owners, 2 * freq_local, lanes), ("x", "z", "low"), 0, 0, tiled=True
    )

    levels = lax.iota(jnp.int32, band_gain.shape[0])
    own_bins = lax.dynamic_slice_in_dim(fk_bins, pair * freq_local, freq_local, 0)
    ordered = own_bins.reshape(freq_local, width, tiles).transpose(2, 0, 1)
    gains = jnp.sum(jnp.where(ordered[..., None] == levels, band_gain, 0.0), axis=-1)
    gains = jnp.concatenate([gains, gains], axis=-1).reshape(tiles * freq_local, lanes)
    residue = lax.iota(jnp.int32, tiles)
    own_blocks = (high * pairs + lax.iota(jnp.int32, pairs)) * cores + core
    recv = own_blocks[:, None] * width + lax.iota(jnp.int32, width)[None, :]
    angle = (residue[None, :, None] * recv[:, None, :] % recv_count).astype(jnp.float32) * (
        2.0 * math.pi / recv_count
    )
    cosine, sine = jnp.cos(angle), jnp.sin(angle)
    unturn = jnp.stack(
        [jnp.concatenate([cosine, cosine], axis=2), jnp.concatenate([-sine, sine], axis=2)],
        axis=1,
    )
    lag = day * lag_local + lax.iota(jnp.int32, lag_local)
    freq = np.arange(freq_count, dtype=np.int32).reshape(depth, breadth, -1)
    freq = jnp.asarray(freq.transpose(1, 0, 2).reshape(-1))
    angle = (lag[:, None] * freq[None, :] % lag_count).astype(jnp.float32) * (
        2.0 * math.pi / lag_count
    )
    weight = jnp.where(freq == 0, 1.0, 2.0).astype(jnp.float32)[None, :] / math.sqrt(lag_count)
    inverse_table = jnp.concatenate([weight * jnp.cos(angle), -weight * jnp.sin(angle)], axis=0)
    table_high = lax.reduce_precision(inverse_table, 8, 7)
    inverse_table = jnp.concatenate([table_high, inverse_table - table_high], axis=0)
    inverse_table = inverse_table.astype(jnp.bfloat16)
    parts, gains, unturn, inverse_table = lax.optimization_barrier(
        (parts, gains, unturn, inverse_table)
    )

    stacked = pl.pallas_call(
        functools.partial(stack_kernel, 1.0 / days),
        in_specs=[VMEM],
        out_specs=VMEM,
        compiler_params=PARAMS,
        out_shape=jax.ShapeDtypeStruct(
            (highs * cores, pairs, 2 * freq_local, lanes), jnp.bfloat16
        ),
    )(parts.reshape(days, pairs, 2 * freq_local, lanes))
    scale = 1.0 / math.sqrt(recv_count)
    turn_angle = np.arange(tiles)[:, None] * np.arange(width)[None, :] * (2.0 * np.pi / recv_count)
    turn = np.stack(
        [
            halves(np.cos(turn_angle), np.cos(turn_angle)),
            halves(np.sin(turn_angle), -np.sin(turn_angle)),
        ]
    )
    gathered = lax.all_to_all(stacked, ("core", "high"), 0, 0, tiled=True)
    lines = pl.pallas_call(
        filter_kernel,
        in_specs=[VMEM] * 6,
        out_specs=VMEM,
        compiler_params=PARAMS,
        out_shape=jax.ShapeDtypeStruct((owners, freq_local, lanes), jnp.bfloat16),
        scratch_shapes=[pltpu.VMEM((tiles * freq_local, lanes), jnp.float32)],
    )(
        gathered,
        gains,
        jnp.asarray(split_rows(block_dft(width, -1.0, scale))),
        jnp.asarray(split_rows(block_dft(width, 1.0, scale))),
        jnp.asarray(turn),
        unturn,
    )
    returned = lax.all_to_all(
        lines, ("x", "z", "low"), 0, 0, tiled=True
    )
    filtered = pl.pallas_call(
        gather_kernel,
        in_specs=[VMEM] * 2,
        out_specs=VMEM,
        compiler_params=PARAMS,
        out_shape=jax.ShapeDtypeStruct((lag_local, width), jnp.float32),
    )(returned, inverse_table)
    return filtered.reshape(lag_local, 1, width)


def solution(mesh):
    days, tiles = mesh.devices.shape
    split = Mesh(mesh.devices.reshape(days // 4, 4, tiles // 2, 1, 2), AXES)
    day, tile = ("z", "x"), ("high", "low", "core")
    return jax.shard_map(
        body,
        mesh=split,
        in_specs=(P(day, None, tile, None), P(day, None, tile, None), P(day, None), P()),
        out_specs=P(day, None, tile),
        check_vma=False,
    )
```

```python
import functools
import math

import jax
import jax.numpy as jnp
import numpy as np
from jax import lax
from jax.experimental import pallas as pl
from jax.experimental.pallas import tpu as pltpu
from jax.sharding import Mesh
from jax.sharding import PartitionSpec as P

AXES = ("z", "x", "high", "low", "core")
SCALE = 2.0**46
TINY = 2.0**-125
VMEM = pl.BlockSpec(memory_space=pltpu.VMEM)
HBM = pl.BlockSpec(memory_space=pltpu.HBM)
PARAMS = pltpu.CompilerParams(vmem_limit_bytes=8 * 2**20)


def lag_basis(freq_count, lag_count, owners):
    freq = np.arange(freq_count)
    phase = (freq[:, None] * np.arange(lag_count)[None, :] % lag_count) * (2.0 * np.pi / lag_count)
    table = np.stack([np.cos(phase), -np.sin(phase)], axis=0) / math.sqrt(lag_count)
    table = table[:, :, : lag_count // 2].reshape(2, owners, freq_count // owners, lag_count // 2)
    table = table.transpose(1, 0, 2, 3).reshape(2 * freq_count, lag_count // 2)
    return table.astype(np.float32).astype(jnp.bfloat16)


def halves(real_part, imag_part):
    return np.concatenate([real_part, imag_part], axis=-1).astype(np.float32)


def block_dft(width, sign, scale):
    angle = (np.arange(width)[:, None] * np.arange(width)[None, :] % width) * (2.0 * np.pi / width)
    cosine, sine = np.cos(angle) * scale, sign * np.sin(angle) * scale
    return np.concatenate([halves(cosine, sine), halves(-sine, cosine)], axis=0)


def other_half(value):
    return pltpu.roll(value, value.shape[-1] // 2, value.ndim - 1)


def lag_kernel(
    table_hbm, causal_hbm, held_hbm, out_ref, table_ref, rows_ref, sems
):
    pieces = sems.shape[0] - 2
    width = causal_hbm.shape[0]
    size = table_ref.shape[0] // pieces
    half = table_ref.shape[1]
    inputs = [
        pltpu.make_async_copy(causal_hbm, rows_ref.at[pl.ds(0, width)], sems.at[pieces]),
        pltpu.make_async_copy(held_hbm, rows_ref.at[pl.ds(width, width)], sems.at[pieces + 1]),
    ]
    tables = [
        pltpu.make_async_copy(
            table_hbm.at[pl.ds(p * size, size)], table_ref.at[pl.ds(p * size, size)], sems.at[p]
        )
        for p in range(pieces)
    ]
    for copy in inputs + tables:
        copy.start()
    for copy in inputs:
        copy.wait()
    rows = rows_ref[...]
    sides = jnp.concatenate([rows[:, :half], rows[:, half:]], axis=0)
    lanes = 2 * width
    odd = lax.broadcasted_iota(jnp.int32, (size, lanes), 0) % 2
    sign = (1 - 2 * odd).astype(jnp.float32)
    for p in range(pieces):
        tables[p].wait()
        both = lax.dot_general(
            table_ref[p * size : (p + 1) * size],
            sides,
            (((1,), (1,)), ((), ())),
            preferred_element_type=jnp.float32,
        )
        out_ref[p * size : (p + 1) * size] = coded(both[:, :lanes] + sign * both[:, lanes:])


def coded(value):
    value = value * SCALE
    return (value * jnp.abs(value)).astype(jnp.bfloat16)


def decoded(code):
    code = code.astype(jnp.float32)
    return code * lax.rsqrt(jnp.maximum(jnp.abs(code), TINY)) * (1.0 / SCALE)


def split(value):
    high = value.astype(jnp.bfloat16)
    return high, (value - high.astype(jnp.float32)).astype(jnp.bfloat16)


def split_rows(matrix):
    high = matrix.astype(jnp.bfloat16)
    low = (matrix - high.astype(np.float32)).astype(jnp.bfloat16)
    return np.concatenate([high, high, low], axis=0)


def product(value, matrix):
    high, low = split(value)
    return jnp.dot(
        jnp.concatenate([high, low, high], axis=1), matrix, preferred_element_type=jnp.float32
    )


def stack_kernel(scale, parts_ref, out_ref):
    count, pairs = parts_ref.shape[0], parts_ref.shape[1]
    half = parts_ref.shape[2] // 2
    totals = [decoded(parts_ref[0, pair]) for pair in range(pairs)]
    for day in range(1, count):
        totals = [totals[pair] + decoded(parts_ref[day, pair]) for pair in range(pairs)]
    for pair in range(pairs):
        total = totals[pair] * scale
        real_part, imag_part = total[:half], total[half:]
        low = lax.broadcasted_iota(jnp.int32, real_part.shape, 1) < real_part.shape[1] // 2
        causal = jnp.where(low, real_part, other_half(imag_part))
        held = jnp.where(low, other_half(real_part), imag_part)
        code = coded(jnp.concatenate([causal, held], axis=0))
        for peer in range(out_ref.shape[0]):
            out_ref[peer, pair] = code


def filter_kernel(
    lines_ref, gains_ref, fore_ref, back_ref, turn_ref, unturn_ref, out_ref, work_ref
):
    peers, pairs, half, lanes = lines_ref.shape
    half //= 2
    blocks = peers * pairs
    low = lax.broadcasted_iota(jnp.int32, (half, lanes), 1) < lanes // 2
    sign = jnp.where(low, 1.0, -1.0)

    def minus_i(value):
        return other_half(value) * sign

    def rotated(value, power):
        power %= 16
        if power == 0:
            return value
        cosine, sine = math.cos(math.pi * power / 8), math.sin(math.pi * power / 8)
        return value * cosine + minus_i(value) * sine

    def four(a, b, c, d):
        p, m, q, n = a + c, a - c, b + d, minus_i(b - d)
        return p + q, m + n, p - q, m - n

    data = []
    value = decoded(lines_ref[...])
    for block in range(blocks):
        high, pair, core = block // (2 * pairs), block // 2 % pairs, block % 2
        highs = peers // 2
        peer, other = core * highs + high, core * highs + (high + highs // 2) % highs
        data.append(value[peer, pair, :half] + value[other, pair, half:])
    inner = [four(*(data[4 * a + b] for a in range(4))) for b in range(4)]
    for c in range(4):
        outer = four(*(rotated(inner[b][c], b * c) for b in range(4)))
        for d in range(4):
            q = c + 4 * d
            value = outer[d]
            work_ref[q * half : (q + 1) * half] = (
                value * turn_ref[0, q : q + 1] + other_half(value) * turn_ref[1, q : q + 1]
            )
    wave = product(work_ref[...], fore_ref[...])
    work_ref[...] = product(wave * gains_ref[...], back_ref[...])
    for pair in range(pairs):
        total = None
        for q in range(blocks):
            value = work_ref[q * half : (q + 1) * half]
            term = value * unturn_ref[pair, 0, q : q + 1] + other_half(value) * unturn_ref[
                pair, 1, q : q + 1
            ]
            total = term if total is None else total + term
        code = coded(total)
        for day in range(out_ref.shape[0] // pairs):
            out_ref[day * pairs + pair] = code


def gather_kernel(codes_ref, table_ref, out_ref):
    owners, freqs, lanes = codes_ref.shape
    rows, width = table_ref.shape[0] // 4, lanes // 2
    chunks = 2
    size = owners // chunks
    total = None
    for c in range(chunks):
        lines = decoded(codes_ref[c * size : (c + 1) * size]).reshape(size * freqs, lanes)
        line_high = lines.astype(jnp.bfloat16)
        table = table_ref[:, c * size * freqs : (c + 1) * size * freqs]
        both = jnp.dot(table, line_high, preferred_element_type=jnp.float32)
        both = both[: 2 * rows] + both[2 * rows :]
        total = both if total is None else total + both
    out_ref[...] = total[:rows, :width] + other_half(total[rows:])[:, :width]


def body(causal, acausal_held, fk_bins, band_gain):
    _, _, width, lag_count = causal.shape
    depth, breadth, highs, pairs, cores = (lax.axis_size(name) for name in AXES)
    days = depth * breadth
    tiles = highs * pairs * cores
    owners = days * pairs
    freq_count = lag_count // 2
    freq_local = freq_count // owners
    recv_count = width * tiles
    lag_local = lag_count // days
    lanes = 2 * width
    z, x, high, pair, core = (lax.axis_index(name) for name in AXES)
    day = z * breadth + x

    table = jnp.asarray(lag_basis(freq_count, lag_count, owners))
    pieces = 1
    spectra = pl.pallas_call(
        lag_kernel,
        in_specs=[HBM] * 3,
        out_specs=VMEM,
        compiler_params=PARAMS,
        out_shape=pltpu.VMEM((2 * freq_count, lanes), jnp.bfloat16),
        scratch_shapes=[
            pltpu.VMEM((2 * freq_count, lag_count // 2), jnp.bfloat16),
            pltpu.VMEM((lanes, lag_count), jnp.bfloat16),
            pltpu.SemaphoreType.DMA((pieces + 2,)),
        ],
    )(
        *(
            pltpu.with_memory_space_constraint(operand, pltpu.HBM)
            for operand in (
                table,
                causal.reshape(width, lag_count),
                acausal_held.reshape(width, lag_count),
            )
        )
    )
    parts = lax.all_to_all(
        spectra.reshape(owners, 2 * freq_local, lanes), ("z", "x", "low"), 0, 0, tiled=True
    )

    levels = lax.iota(jnp.int32, band_gain.shape[0])
    own_bins = lax.dynamic_slice_in_dim(fk_bins, pair * freq_local, freq_local, 0)
    ordered = own_bins.reshape(freq_local, width, tiles).transpose(2, 0, 1)
    gains = jnp.sum(jnp.where(ordered[..., None] == levels, band_gain, 0.0), axis=-1)
    gains = jnp.concatenate([gains, gains], axis=-1).reshape(tiles * freq_local, lanes)
    residue = lax.iota(jnp.int32, tiles)
    own_blocks = (high * pairs + lax.iota(jnp.int32, pairs)) * cores + core
    recv = own_blocks[:, None] * width + lax.iota(jnp.int32, width)[None, :]
    angle = (residue[None, :, None] * recv[:, None, :] % recv_count).astype(jnp.float32) * (
        2.0 * math.pi / recv_count
    )
    cosine, sine = jnp.cos(angle), jnp.sin(angle)
    unturn = jnp.stack(
        [jnp.concatenate([cosine, cosine], axis=2), jnp.concatenate([-sine, sine], axis=2)],
        axis=1,
    )
    lag = day * lag_local + lax.iota(jnp.int32, lag_local)
    freq = np.arange(freq_count, dtype=np.int32).reshape(depth, breadth, -1)
    freq = jnp.asarray(freq.transpose(1, 0, 2).reshape(-1))
    angle = (lag[:, None] * freq[None, :] % lag_count).astype(jnp.float32) * (
        2.0 * math.pi / lag_count
    )
    weight = jnp.where(freq == 0, 1.0, 2.0).astype(jnp.float32)[None, :] / math.sqrt(lag_count)
    inverse_table = jnp.concatenate([weight * jnp.cos(angle), -weight * jnp.sin(angle)], axis=0)
    table_high = lax.reduce_precision(inverse_table, 8, 7)
    inverse_table = jnp.concatenate([table_high, inverse_table - table_high], axis=0)
    inverse_table = inverse_table.astype(jnp.bfloat16)
    parts, gains, unturn, inverse_table = lax.optimization_barrier(
        (parts, gains, unturn, inverse_table)
    )

    stacked = pl.pallas_call(
        functools.partial(stack_kernel, 1.0 / days),
        in_specs=[VMEM],
        out_specs=VMEM,
        compiler_params=PARAMS,
        out_shape=jax.ShapeDtypeStruct(
            (highs * cores, pairs, 2 * freq_local, lanes), jnp.bfloat16
        ),
    )(parts.reshape(days, pairs, 2 * freq_local, lanes))
    scale = 1.0 / math.sqrt(recv_count)
    turn_angle = np.arange(tiles)[:, None] * np.arange(width)[None, :] * (2.0 * np.pi / recv_count)
    turn = np.stack(
        [
            halves(np.cos(turn_angle), np.cos(turn_angle)),
            halves(np.sin(turn_angle), -np.sin(turn_angle)),
        ]
    )
    gathered = lax.all_to_all(stacked, ("core", "high"), 0, 0, tiled=True)
    lines = pl.pallas_call(
        filter_kernel,
        in_specs=[VMEM] * 6,
        out_specs=VMEM,
        compiler_params=PARAMS,
        out_shape=jax.ShapeDtypeStruct((owners, freq_local, lanes), jnp.bfloat16),
        scratch_shapes=[pltpu.VMEM((tiles * freq_local, lanes), jnp.float32)],
    )(
        gathered,
        gains,
        jnp.asarray(split_rows(block_dft(width, -1.0, scale))),
        jnp.asarray(split_rows(block_dft(width, 1.0, scale))),
        jnp.asarray(turn),
        unturn,
    )
    returned = lax.all_to_all(
        lines, ("x", "z", "low"), 0, 0, tiled=True
    )
    filtered = pl.pallas_call(
        gather_kernel,
        in_specs=[VMEM] * 2,
        out_specs=VMEM,
        compiler_params=PARAMS,
        out_shape=jax.ShapeDtypeStruct((lag_local, width), jnp.float32),
    )(returned, inverse_table)
    return filtered.reshape(lag_local, 1, width)


def solution(mesh):
    days, tiles = mesh.devices.shape
    split = Mesh(mesh.devices.reshape(days // 4, 4, tiles // 2, 1, 2), AXES)
    day, tile = ("z", "x"), ("high", "low", "core")
    return jax.shard_map(
        body,
        mesh=split,
        in_specs=(P(day, None, tile, None), P(day, None, tile, None), P(day, None), P()),
        out_specs=P(day, None, tile),
        check_vma=False,
    )
```

```python
import functools
import math

import jax
import jax.numpy as jnp
import numpy as np
from jax import lax
from jax.experimental import pallas as pl
from jax.experimental.pallas import tpu as pltpu
from jax.sharding import Mesh
from jax.sharding import PartitionSpec as P

AXES = ("z", "x", "high", "low", "core")
SCALE = 2.0**46
TINY = 2.0**-125
VMEM = pl.BlockSpec(memory_space=pltpu.VMEM)
HBM = pl.BlockSpec(memory_space=pltpu.HBM)
PARAMS = pltpu.CompilerParams(vmem_limit_bytes=8 * 2**20)


def lag_basis(freq_count, lag_count, owners):
    freq = np.arange(freq_count)
    phase = (freq[:, None] * np.arange(lag_count)[None, :] % lag_count) * (2.0 * np.pi / lag_count)
    table = np.stack([np.cos(phase), -np.sin(phase)], axis=0) / math.sqrt(lag_count)
    table = table[:, :, : lag_count // 2].reshape(2, owners, freq_count // owners, lag_count // 2)
    table = table.transpose(1, 0, 2, 3).reshape(2 * freq_count, lag_count // 2)
    return table.astype(np.float32).astype(jnp.bfloat16)


def halves(real_part, imag_part):
    return np.concatenate([real_part, imag_part], axis=-1).astype(np.float32)


def block_dft(width, sign, scale):
    angle = (np.arange(width)[:, None] * np.arange(width)[None, :] % width) * (2.0 * np.pi / width)
    cosine, sine = np.cos(angle) * scale, sign * np.sin(angle) * scale
    return np.concatenate([halves(cosine, sine), halves(-sine, cosine)], axis=0)


def other_half(value):
    return pltpu.roll(value, value.shape[-1] // 2, value.ndim - 1)


def lag_kernel(
    table_hbm, causal_hbm, held_hbm, out_ref, table_ref, rows_ref, sems
):
    pieces = sems.shape[0] - 2
    width = causal_hbm.shape[0]
    size = table_ref.shape[0] // pieces
    half = table_ref.shape[1]
    inputs = [
        pltpu.make_async_copy(causal_hbm, rows_ref.at[pl.ds(0, width)], sems.at[pieces]),
        pltpu.make_async_copy(held_hbm, rows_ref.at[pl.ds(width, width)], sems.at[pieces + 1]),
    ]
    tables = [
        pltpu.make_async_copy(
            table_hbm.at[pl.ds(p * size, size)], table_ref.at[pl.ds(p * size, size)], sems.at[p]
        )
        for p in range(pieces)
    ]
    for copy in inputs + tables:
        copy.start()
    for copy in inputs:
        copy.wait()
    rows = rows_ref[...]
    sides = jnp.concatenate([rows[:, :half], rows[:, half:]], axis=0)
    lanes = 2 * width
    odd = lax.broadcasted_iota(jnp.int32, (size, lanes), 0) % 2
    sign = (1 - 2 * odd).astype(jnp.float32)
    for p in range(pieces):
        tables[p].wait()
        both = lax.dot_general(
            table_ref[p * size : (p + 1) * size],
            sides,
            (((1,), (1,)), ((), ())),
            preferred_element_type=jnp.float32,
        )
        out_ref[p * size : (p + 1) * size] = coded(both[:, :lanes] + sign * both[:, lanes:])


def coded(value):
    value = value * SCALE
    return (value * jnp.abs(value)).astype(jnp.bfloat16)


def decoded(code):
    code = code.astype(jnp.float32)
    return code * lax.rsqrt(jnp.maximum(jnp.abs(code), TINY)) * (1.0 / SCALE)


def split(value):
    high = value.astype(jnp.bfloat16)
    return high, (value - high.astype(jnp.float32)).astype(jnp.bfloat16)


def split_rows(matrix):
    high = matrix.astype(jnp.bfloat16)
    low = (matrix - high.astype(np.float32)).astype(jnp.bfloat16)
    return np.concatenate([high, high, low], axis=0)


def product(value, matrix):
    high, low = split(value)
    return jnp.dot(
        jnp.concatenate([high, low, high], axis=1), matrix, preferred_element_type=jnp.float32
    )


def stack_kernel(scale, parts_ref, out_ref):
    count, pairs = parts_ref.shape[0], parts_ref.shape[1]
    half = parts_ref.shape[2] // 2
    totals = [decoded(parts_ref[0, pair]) for pair in range(pairs)]
    for day in range(1, count):
        totals = [totals[pair] + decoded(parts_ref[day, pair]) for pair in range(pairs)]
    for pair in range(pairs):
        total = totals[pair] * scale
        real_part, imag_part = total[:half], total[half:]
        low = lax.broadcasted_iota(jnp.int32, real_part.shape, 1) < real_part.shape[1] // 2
        causal = jnp.where(low, real_part, other_half(imag_part))
        held = jnp.where(low, other_half(real_part), imag_part)
        code = coded(jnp.concatenate([causal, held], axis=0))
        for peer in range(out_ref.shape[0]):
            out_ref[peer, pair] = code


def filter_kernel(
    lines_ref, gains_ref, fore_ref, back_ref, turn_ref, unturn_ref, out_ref, work_ref
):
    peers, pairs, half, lanes = lines_ref.shape
    half //= 2
    blocks = peers * pairs
    low = lax.broadcasted_iota(jnp.int32, (half, lanes), 1) < lanes // 2
    sign = jnp.where(low, 1.0, -1.0)

    def minus_i(value):
        return other_half(value) * sign

    def rotated(value, power):
        power %= 16
        if power == 0:
            return value
        cosine, sine = math.cos(math.pi * power / 8), math.sin(math.pi * power / 8)
        return value * cosine + minus_i(value) * sine

    def four(a, b, c, d):
        p, m, q, n = a + c, a - c, b + d, minus_i(b - d)
        return p + q, m + n, p - q, m - n

    data = []
    value = decoded(lines_ref[...])
    for block in range(blocks):
        high, pair, core = block // (2 * pairs), block // 2 % pairs, block % 2
        highs = peers // 2
        peer, other = core * highs + high, core * highs + (high + highs // 2) % highs
        data.append(value[peer, pair, :half] + value[other, pair, half:])
    inner = [four(*(data[4 * a + b] for a in range(4))) for b in range(4)]
    for c in range(4):
        outer = four(*(rotated(inner[b][c], b * c) for b in range(4)))
        for d in range(4):
            q = c + 4 * d
            value = outer[d]
            work_ref[q * half : (q + 1) * half] = (
                value * turn_ref[0, q : q + 1] + other_half(value) * turn_ref[1, q : q + 1]
            )
    wave = product(work_ref[...], fore_ref[...])
    work_ref[...] = product(wave * gains_ref[...], back_ref[...])
    for pair in range(pairs):
        total = None
        for q in range(blocks):
            value = work_ref[q * half : (q + 1) * half]
            term = value * unturn_ref[pair, 0, q : q + 1] + other_half(value) * unturn_ref[
                pair, 1, q : q + 1
            ]
            total = term if total is None else total + term
        code = coded(total)
        for day in range(out_ref.shape[0] // pairs):
            out_ref[day * pairs + pair] = code


def gather_kernel(codes_ref, table_ref, out_ref):
    owners, freqs, lanes = codes_ref.shape
    rows, width = table_ref.shape[0] // 4, lanes // 2
    chunks = 2
    size = owners // chunks
    total = None
    for c in range(chunks):
        lines = decoded(codes_ref[c * size : (c + 1) * size]).reshape(size * freqs, lanes)
        line_high, line_low = split(lines)
        table = table_ref[:, c * size * freqs : (c + 1) * size * freqs]
        both = jnp.dot(table, line_high, preferred_element_type=jnp.float32)
        both = both[: 2 * rows] + both[2 * rows :]
        both = both + jnp.dot(table[: 2 * rows], line_low, preferred_element_type=jnp.float32)
        total = both if total is None else total + both
    out_ref[...] = total[:rows, :width] + other_half(total[rows:])[:, :width]


def body(causal, acausal_held, fk_bins, band_gain):
    _, _, width, lag_count = causal.shape
    depth, breadth, highs, pairs, cores = (lax.axis_size(name) for name in AXES)
    days = depth * breadth
    tiles = highs * pairs * cores
    owners = days * pairs
    freq_count = lag_count // 2
    freq_local = freq_count // owners
    recv_count = width * tiles
    lag_local = lag_count // days
    lanes = 2 * width
    z, x, high, pair, core = (lax.axis_index(name) for name in AXES)
    day = z * breadth + x

    table = jnp.asarray(lag_basis(freq_count, lag_count, owners))
    pieces = 1
    spectra = pl.pallas_call(
        lag_kernel,
        in_specs=[HBM] * 3,
        out_specs=VMEM,
        compiler_params=PARAMS,
        out_shape=pltpu.VMEM((2 * freq_count, lanes), jnp.bfloat16),
        scratch_shapes=[
            pltpu.VMEM((2 * freq_count, lag_count // 2), jnp.bfloat16),
            pltpu.VMEM((lanes, lag_count), jnp.bfloat16),
            pltpu.SemaphoreType.DMA((pieces + 2,)),
        ],
    )(
        *(
            pltpu.with_memory_space_constraint(operand, pltpu.HBM)
            for operand in (
                table,
                causal.reshape(width, lag_count),
                acausal_held.reshape(width, lag_count),
            )
        )
    )
    parts = lax.all_to_all(
        spectra.reshape(owners, 2 * freq_local, lanes), ("z", "x", "low"), 0, 0, tiled=True
    )

    levels = lax.iota(jnp.int32, band_gain.shape[0])
    own_bins = lax.dynamic_slice_in_dim(fk_bins, pair * freq_local, freq_local, 0)
    ordered = own_bins.reshape(freq_local, width, tiles).transpose(2, 0, 1)
    gains = jnp.sum(jnp.where(ordered[..., None] == levels, band_gain, 0.0), axis=-1)
    gains = jnp.concatenate([gains, gains], axis=-1).reshape(tiles * freq_local, lanes)
    residue = lax.iota(jnp.int32, tiles)
    own_blocks = (high * pairs + lax.iota(jnp.int32, pairs)) * cores + core
    recv = own_blocks[:, None] * width + lax.iota(jnp.int32, width)[None, :]
    angle = (residue[None, :, None] * recv[:, None, :] % recv_count).astype(jnp.float32) * (
        2.0 * math.pi / recv_count
    )
    cosine, sine = jnp.cos(angle), jnp.sin(angle)
    unturn = jnp.stack(
        [jnp.concatenate([cosine, cosine], axis=2), jnp.concatenate([-sine, sine], axis=2)],
        axis=1,
    )
    lag = day * lag_local + lax.iota(jnp.int32, lag_local)
    freq = np.arange(freq_count, dtype=np.int32).reshape(depth, breadth, -1)
    freq = jnp.asarray(freq.transpose(1, 0, 2).reshape(-1))
    angle = (lag[:, None] * freq[None, :] % lag_count).astype(jnp.float32) * (
        2.0 * math.pi / lag_count
    )
    weight = jnp.where(freq == 0, 1.0, 2.0).astype(jnp.float32)[None, :] / math.sqrt(lag_count)
    inverse_table = jnp.concatenate([weight * jnp.cos(angle), -weight * jnp.sin(angle)], axis=0)
    table_high = lax.reduce_precision(inverse_table, 8, 7)
    inverse_table = jnp.concatenate([table_high, inverse_table - table_high], axis=0)
    inverse_table = inverse_table.astype(jnp.bfloat16)
    parts, gains, unturn, inverse_table = lax.optimization_barrier(
        (parts, gains, unturn, inverse_table)
    )

    stacked = pl.pallas_call(
        functools.partial(stack_kernel, 1.0 / days),
        in_specs=[VMEM],
        out_specs=VMEM,
        compiler_params=PARAMS,
        out_shape=jax.ShapeDtypeStruct(
            (highs * cores, pairs, 2 * freq_local, lanes), jnp.bfloat16
        ),
    )(parts.reshape(days, pairs, 2 * freq_local, lanes))
    scale = 1.0 / math.sqrt(recv_count)
    turn_angle = np.arange(tiles)[:, None] * np.arange(width)[None, :] * (2.0 * np.pi / recv_count)
    turn = np.stack(
        [
            halves(np.cos(turn_angle), np.cos(turn_angle)),
            halves(np.sin(turn_angle), -np.sin(turn_angle)),
        ]
    )
    gathered = lax.all_to_all(stacked, ("core", "high"), 0, 0, tiled=True)
    lines = pl.pallas_call(
        filter_kernel,
        in_specs=[VMEM] * 6,
        out_specs=VMEM,
        compiler_params=PARAMS,
        out_shape=jax.ShapeDtypeStruct((owners, freq_local, lanes), jnp.bfloat16),
        scratch_shapes=[pltpu.VMEM((tiles * freq_local, lanes), jnp.float32)],
    )(
        gathered,
        gains,
        jnp.asarray(split_rows(block_dft(width, -1.0, scale))),
        jnp.asarray(split_rows(block_dft(width, 1.0, scale))),
        jnp.asarray(turn),
        unturn,
    )
    returned = lax.all_to_all(
        lines, ("x", "z", "low"), 0, 0, tiled=True
    )
    filtered = pl.pallas_call(
        gather_kernel,
        in_specs=[VMEM] * 2,
        out_specs=VMEM,
        compiler_params=PARAMS,
        out_shape=jax.ShapeDtypeStruct((lag_local, width), jnp.float32),
    )(returned, inverse_table)
    return filtered.reshape(lag_local, 1, width)


def solution(mesh):
    days, tiles = mesh.devices.shape
    split = Mesh(mesh.devices.reshape(days // 4, 4, tiles // 4, 2, 2), AXES)
    day, tile = ("z", "x"), ("high", "low", "core")
    return jax.shard_map(
        body,
        mesh=split,
        in_specs=(P(day, None, tile, None), P(day, None, tile, None), P(day, None), P()),
        out_specs=P(day, None, tile),
        check_vma=False,
    )
```

```python
import functools
import math

import jax
import jax.numpy as jnp
import numpy as np
from jax import lax
from jax.experimental import pallas as pl
from jax.experimental.pallas import tpu as pltpu
from jax.sharding import Mesh
from jax.sharding import PartitionSpec as P

AXES = ("z", "x", "high", "low", "core")
SCALE = 2.0**46
TINY = 2.0**-125
VMEM = pl.BlockSpec(memory_space=pltpu.VMEM)
HBM = pl.BlockSpec(memory_space=pltpu.HBM)
PARAMS = pltpu.CompilerParams(vmem_limit_bytes=8 * 2**20)


def lag_basis(freq_count, lag_count, owners):
    freq = np.arange(freq_count)
    phase = (freq[:, None] * np.arange(lag_count)[None, :] % lag_count) * (2.0 * np.pi / lag_count)
    table = np.stack([np.cos(phase), -np.sin(phase)], axis=0) / math.sqrt(lag_count)
    table = table[:, :, : lag_count // 2].reshape(2, owners, freq_count // owners, lag_count // 2)
    table = table.transpose(1, 0, 2, 3).reshape(2 * freq_count, lag_count // 2)
    return table.astype(np.float32).astype(jnp.bfloat16)


def halves(real_part, imag_part):
    return np.concatenate([real_part, imag_part], axis=-1).astype(np.float32)


def block_dft(width, sign, scale):
    angle = (np.arange(width)[:, None] * np.arange(width)[None, :] % width) * (2.0 * np.pi / width)
    cosine, sine = np.cos(angle) * scale, sign * np.sin(angle) * scale
    return np.concatenate([halves(cosine, sine), halves(-sine, cosine)], axis=0)


def other_half(value):
    return pltpu.roll(value, value.shape[-1] // 2, value.ndim - 1)


def lag_kernel(
    table_hbm, causal_hbm, held_hbm, out_ref, table_ref, rows_ref, sems
):
    pieces = sems.shape[0] - 2
    width = causal_hbm.shape[0]
    size = table_ref.shape[0] // pieces
    half = table_ref.shape[1]
    inputs = [
        pltpu.make_async_copy(causal_hbm, rows_ref.at[pl.ds(0, width)], sems.at[pieces]),
        pltpu.make_async_copy(held_hbm, rows_ref.at[pl.ds(width, width)], sems.at[pieces + 1]),
    ]
    tables = [
        pltpu.make_async_copy(
            table_hbm.at[pl.ds(p * size, size)], table_ref.at[pl.ds(p * size, size)], sems.at[p]
        )
        for p in range(pieces)
    ]
    for copy in inputs + tables:
        copy.start()
    for copy in inputs:
        copy.wait()
    rows = rows_ref[...]
    sides = jnp.concatenate([rows[:, :half], rows[:, half:]], axis=0)
    lanes = 2 * width
    odd = lax.broadcasted_iota(jnp.int32, (size, lanes), 0) % 2
    sign = (1 - 2 * odd).astype(jnp.float32)
    for p in range(pieces):
        tables[p].wait()
        both = lax.dot_general(
            table_ref[p * size : (p + 1) * size],
            sides,
            (((1,), (1,)), ((), ())),
            preferred_element_type=jnp.float32,
        )
        out_ref[p * size : (p + 1) * size] = coded(both[:, :lanes] + sign * both[:, lanes:])


def coded(value):
    value = value * SCALE
    return (value * jnp.abs(value)).astype(jnp.bfloat16)


def decoded(code):
    code = code.astype(jnp.float32)
    return code * lax.rsqrt(jnp.maximum(jnp.abs(code), TINY)) * (1.0 / SCALE)


def split(value):
    high = value.astype(jnp.bfloat16)
    return high, (value - high.astype(jnp.float32)).astype(jnp.bfloat16)


def split_rows(matrix):
    high = matrix.astype(jnp.bfloat16)
    low = (matrix - high.astype(np.float32)).astype(jnp.bfloat16)
    return np.concatenate([high, high, low], axis=0)


def product(value, matrix):
    high, low = split(value)
    return jnp.dot(
        jnp.concatenate([high, low, high], axis=1), matrix, preferred_element_type=jnp.float32
    )


def stack_kernel(scale, parts_ref, out_ref):
    count, pairs = parts_ref.shape[0], parts_ref.shape[1]
    half = parts_ref.shape[2] // 2
    totals = [decoded(parts_ref[0, pair]) for pair in range(pairs)]
    for day in range(1, count):
        totals = [totals[pair] + decoded(parts_ref[day, pair]) for pair in range(pairs)]
    for pair in range(pairs):
        total = totals[pair] * scale
        real_part, imag_part = total[:half], total[half:]
        low = lax.broadcasted_iota(jnp.int32, real_part.shape, 1) < real_part.shape[1] // 2
        causal = jnp.where(low, real_part, other_half(imag_part))
        held = jnp.where(low, other_half(real_part), imag_part)
        code = coded(jnp.concatenate([causal, held], axis=0))
        for peer in range(out_ref.shape[0]):
            out_ref[peer, pair] = code


def filter_kernel(
    lines_ref, gains_ref, fore_ref, back_ref, turn_ref, unturn_ref, out_ref, work_ref
):
    peers, pairs, half, lanes = lines_ref.shape
    half //= 2
    blocks = peers * pairs
    low = lax.broadcasted_iota(jnp.int32, (half, lanes), 1) < lanes // 2
    sign = jnp.where(low, 1.0, -1.0)

    def minus_i(value):
        return other_half(value) * sign

    def rotated(value, power):
        power %= 16
        if power == 0:
            return value
        cosine, sine = math.cos(math.pi * power / 8), math.sin(math.pi * power / 8)
        return value * cosine + minus_i(value) * sine

    def four(a, b, c, d):
        p, m, q, n = a + c, a - c, b + d, minus_i(b - d)
        return p + q, m + n, p - q, m - n

    data = []
    value = decoded(lines_ref[...])
    for block in range(blocks):
        high, pair, core = block // (2 * pairs), block // 2 % pairs, block % 2
        highs = peers // 2
        peer, other = 2 * high + core, 2 * ((high + highs // 2) % highs) + core
        data.append(value[peer, pair, :half] + value[other, pair, half:])
    inner = [four(*(data[4 * a + b] for a in range(4))) for b in range(4)]
    for c in range(4):
        outer = four(*(rotated(inner[b][c], b * c) for b in range(4)))
        for d in range(4):
            q = c + 4 * d
            value = outer[d]
            work_ref[q * half : (q + 1) * half] = (
                value * turn_ref[0, q : q + 1] + other_half(value) * turn_ref[1, q : q + 1]
            )
    wave = product(work_ref[...], fore_ref[...])
    work_ref[...] = product(wave * gains_ref[...], back_ref[...])
    for pair in range(pairs):
        total = None
        for q in range(blocks):
            value = work_ref[q * half : (q + 1) * half]
            term = value * unturn_ref[pair, 0, q : q + 1] + other_half(value) * unturn_ref[
                pair, 1, q : q + 1
            ]
            total = term if total is None else total + term
        code = coded(total)
        for day in range(out_ref.shape[0] // pairs):
            out_ref[day * pairs + pair] = code


def gather_kernel(codes_ref, table_ref, out_ref):
    owners, freqs, lanes = codes_ref.shape
    rows, width = table_ref.shape[0] // 4, lanes // 2
    chunks = 2
    size = owners // chunks
    total = None
    for c in range(chunks):
        lines = decoded(codes_ref[c * size : (c + 1) * size]).reshape(size * freqs, lanes)
        line_high, line_low = split(lines)
        table = table_ref[:, c * size * freqs : (c + 1) * size * freqs]
        both = jnp.dot(table, line_high, preferred_element_type=jnp.float32)
        both = both[: 2 * rows] + both[2 * rows :]
        both = both + jnp.dot(table[: 2 * rows], line_low, preferred_element_type=jnp.float32)
        total = both if total is None else total + both
    out_ref[...] = total[:rows, :width] + other_half(total[rows:])[:, :width]


def body(causal, acausal_held, fk_bins, band_gain):
    _, _, width, lag_count = causal.shape
    depth, breadth, highs, pairs, cores = (lax.axis_size(name) for name in AXES)
    days = depth * breadth
    tiles = highs * pairs * cores
    owners = days * pairs
    freq_count = lag_count // 2
    freq_local = freq_count // owners
    recv_count = width * tiles
    lag_local = lag_count // days
    lanes = 2 * width
    z, x, high, pair, core = (lax.axis_index(name) for name in AXES)
    day = z * breadth + x

    table = jnp.asarray(lag_basis(freq_count, lag_count, owners))
    pieces = 1
    spectra = pl.pallas_call(
        lag_kernel,
        in_specs=[HBM] * 3,
        out_specs=VMEM,
        compiler_params=PARAMS,
        out_shape=pltpu.VMEM((2 * freq_count, lanes), jnp.bfloat16),
        scratch_shapes=[
            pltpu.VMEM((2 * freq_count, lag_count // 2), jnp.bfloat16),
            pltpu.VMEM((lanes, lag_count), jnp.bfloat16),
            pltpu.SemaphoreType.DMA((pieces + 2,)),
        ],
    )(
        *(
            pltpu.with_memory_space_constraint(operand, pltpu.HBM)
            for operand in (
                table,
                causal.reshape(width, lag_count),
                acausal_held.reshape(width, lag_count),
            )
        )
    )
    parts = lax.all_to_all(
        spectra.reshape(owners, 2 * freq_local, lanes), ("z", "x", "low"), 0, 0, tiled=True
    )

    levels = lax.iota(jnp.int32, band_gain.shape[0])
    own_bins = lax.dynamic_slice_in_dim(fk_bins, pair * freq_local, freq_local, 0)
    ordered = own_bins.reshape(freq_local, width, tiles).transpose(2, 0, 1)
    gains = jnp.sum(jnp.where(ordered[..., None] == levels, band_gain, 0.0), axis=-1)
    gains = jnp.concatenate([gains, gains], axis=-1).reshape(tiles * freq_local, lanes)
    residue = lax.iota(jnp.int32, tiles)
    own_blocks = (high * pairs + lax.iota(jnp.int32, pairs)) * cores + core
    recv = own_blocks[:, None] * width + lax.iota(jnp.int32, width)[None, :]
    angle = (residue[None, :, None] * recv[:, None, :] % recv_count).astype(jnp.float32) * (
        2.0 * math.pi / recv_count
    )
    cosine, sine = jnp.cos(angle), jnp.sin(angle)
    unturn = jnp.stack(
        [jnp.concatenate([cosine, cosine], axis=2), jnp.concatenate([-sine, sine], axis=2)],
        axis=1,
    )
    lag = day * lag_local + lax.iota(jnp.int32, lag_local)
    freq = np.arange(freq_count, dtype=np.int32).reshape(depth, breadth, -1)
    freq = jnp.asarray(freq.transpose(1, 0, 2).reshape(-1))
    angle = (lag[:, None] * freq[None, :] % lag_count).astype(jnp.float32) * (
        2.0 * math.pi / lag_count
    )
    weight = jnp.where(freq == 0, 1.0, 2.0).astype(jnp.float32)[None, :] / math.sqrt(lag_count)
    inverse_table = jnp.concatenate([weight * jnp.cos(angle), -weight * jnp.sin(angle)], axis=0)
    table_high = lax.reduce_precision(inverse_table, 8, 7)
    inverse_table = jnp.concatenate([table_high, inverse_table - table_high], axis=0)
    inverse_table = inverse_table.astype(jnp.bfloat16)
    parts, gains, unturn, inverse_table = lax.optimization_barrier(
        (parts, gains, unturn, inverse_table)
    )

    stacked = pl.pallas_call(
        functools.partial(stack_kernel, 1.0 / days),
        in_specs=[VMEM],
        out_specs=VMEM,
        compiler_params=PARAMS,
        out_shape=jax.ShapeDtypeStruct(
            (highs * cores, pairs, 2 * freq_local, lanes), jnp.bfloat16
        ),
    )(parts.reshape(days, pairs, 2 * freq_local, lanes))
    scale = 1.0 / math.sqrt(recv_count)
    turn_angle = np.arange(tiles)[:, None] * np.arange(width)[None, :] * (2.0 * np.pi / recv_count)
    turn = np.stack(
        [
            halves(np.cos(turn_angle), np.cos(turn_angle)),
            halves(np.sin(turn_angle), -np.sin(turn_angle)),
        ]
    )
    gathered = lax.all_to_all(stacked, ("high", "core"), 0, 0, tiled=True)
    lines = pl.pallas_call(
        filter_kernel,
        in_specs=[VMEM] * 6,
        out_specs=VMEM,
        compiler_params=PARAMS,
        out_shape=jax.ShapeDtypeStruct((owners, freq_local, lanes), jnp.bfloat16),
        scratch_shapes=[pltpu.VMEM((tiles * freq_local, lanes), jnp.float32)],
    )(
        gathered,
        gains,
        jnp.asarray(split_rows(block_dft(width, -1.0, scale))),
        jnp.asarray(split_rows(block_dft(width, 1.0, scale))),
        jnp.asarray(turn),
        unturn,
    )
    returned = lax.all_to_all(
        lines, ("x", "z", "low"), 0, 0, tiled=True
    )
    filtered = pl.pallas_call(
        gather_kernel,
        in_specs=[VMEM] * 2,
        out_specs=VMEM,
        compiler_params=PARAMS,
        out_shape=jax.ShapeDtypeStruct((lag_local, width), jnp.float32),
    )(returned, inverse_table)
    return filtered.reshape(lag_local, 1, width)


def solution(mesh):
    days, tiles = mesh.devices.shape
    split = Mesh(mesh.devices.reshape(days // 4, 4, tiles // 2, 1, 2), AXES)
    day, tile = ("z", "x"), ("high", "low", "core")
    return jax.shard_map(
        body,
        mesh=split,
        in_specs=(P(day, None, tile, None), P(day, None, tile, None), P(day, None), P()),
        out_specs=P(day, None, tile),
        check_vma=False,
    )
```
